768 devices in a mesh: dp: 24 (over z, core), seq: 4 (over x), head: 8 (over y).
Axes of the slice: x: 4, y: 8, z: 12, core: 2. Of those that a mesh axis runs over, the one named last changes fastest.
Arguments:
- queries: bfloat16 [24, 1440, 2048], P('dp', 'seq', 'head'), may hold values from -40 to 40
- key_rows: bfloat16 [24, 1440, 1024], P('dp', 'seq', 'head'), may hold values from -6 to 6
- value_rows: bfloat16 [24, 1440, 1024], P('dp', 'seq', 'head'), may hold values from -6 to 6
- grad_out: bfloat16 [24, 1440, 2048], P('dp', 'seq', 'head'), may hold values from -6 to 6
- doc_lengths: int32 [24, 4], P('dp'), may hold values from 2 to 1080, as said below
- dest_index: int32 [24, 1440], P('dp', 'seq'), may hold values from 0 to 23, as said below
Outputs:
- attended: bfloat16 [24, 1440, 2048], P('dp', 'seq', 'head')
- query_grad: bfloat16 [24, 1440, 2048], P('dp', 'seq', 'head')
- key_grad: bfloat16 [24, 1440, 1024], P('dp', 'seq', 'head')
- value_grad: bfloat16 [24, 1440, 1024], P('dp', 'seq', 'head')
The draws below stay inside these ranges and needn't reach their ends.
Inputs may be any that keep to these rules, and one draw needn't show every extreme that they name: `dest_index`: within each loader sequence and each shard of 360 positions, every value 0 to 23 appears exactly 360 / 24 times. `doc_lengths`: each row holds 4 lengths that sum to 1440; the largest is exactly 1080.
All inputs are finite; a program needn't handle non-finite values.
Results may differ from the reference program's by a relative error of at most 0.0095.
Values may be sent and summed in bfloat16 or wider, within the bound.
A program may use at most 32 MiB of HBM per device.

```python
import jax
import jax.numpy as jnp
from jax import lax

HEAD_DIM = 128
QHEADS = 16
KVHEADS = 8
WINDOW = 1024
ROWS = 360
SEQS = 24
LENGTH = 1440
MAXDOC = 1080


def doc_table(key):
    rest = LENGTH - MAXDOC

    def one_row(row_key):
        first_key, second_key, order_key = jax.random.split(row_key, 3)
        first = jax.random.randint(first_key, (), 2, rest // 2, dtype=jnp.int32)
        second = jax.random.randint(second_key, (), 2, rest // 4, dtype=jnp.int32)
        table = jnp.stack([jnp.asarray(MAXDOC, jnp.int32), first, second, rest - first - second])
        return table[jax.random.permutation(order_key, 4)]
    return jax.vmap(one_row)(jax.random.split(jax.random.fold_in(key, 11), SEQS))


def dest_table(key):
    span_count = LENGTH // ROWS
    group_rows = ROWS // SEQS
    row_keys = jax.random.split(jax.random.fold_in(key, 23), SEQS * span_count)
    ranking = jax.vmap(lambda row_key: jax.random.permutation(row_key, ROWS))(row_keys)
    return (ranking // group_rows).reshape(SEQS, LENGTH).astype(jnp.int32)


def draw_queries(key, part):
    shape = (SEQS, LENGTH, QHEADS * HEAD_DIM)
    noise = jax.random.normal(jax.random.fold_in(key, 3), shape, jnp.float32)
    return jnp.clip(2.0 * noise, -8.0, 8.0).astype(jnp.bfloat16)


def draw_key_rows(key, part):
    shape = (SEQS, LENGTH, KVHEADS * HEAD_DIM)
    noise = jax.random.normal(jax.random.fold_in(key, 5), shape, jnp.float32)
    return jnp.clip(noise, -6.0, 6.0).astype(jnp.bfloat16)


def draw_doc_lengths(key, part):
    return doc_table(key)


def draw_dest_index(key, part):
    return dest_table(key)


def steps_of(stream_key, dims, shards, low, high):
    gain, own = 1.0, jax.random.fold_in(stream_key, 6)
    for position, blocks in shards:
        draws = jnp.exp(jax.random.uniform(jax.random.fold_in(own, position), (blocks,), jnp.float32, low / len(shards), high / len(shards)))
        gain = gain * jnp.repeat(draws, dims[position] // blocks).reshape([-1 if axis == position else 1 for axis in range(len(dims))])
    return gain


def scatter_about(key, shape, spread, bound, cuts=(), kind=jnp.bfloat16):
    values = jax.random.normal(key, shape, jnp.float32) * spread
    if len(cuts) > 0:
        values = steps_of(key, shape, cuts, -0.22, 0.18) * values
    return jnp.clip(values, min=-bound, max=bound).astype(kind)


def setup_inputs(seed: int = 0) -> dict:
    key_of = jax.random.split(jax.random.key(seed), 7)
    queries = draw_queries(jax.random.fold_in(key_of[6], 71), 0)
    key_rows = draw_key_rows(jax.random.fold_in(key_of[6], 71), 0)
    value_rows = scatter_about(key_of[2], (SEQS, LENGTH, KVHEADS * HEAD_DIM), 1.0, 6.0, ((0, 24), (1, 4), (2, 8)))
    grad_out = scatter_about(key_of[3], (SEQS, LENGTH, QHEADS * HEAD_DIM), 1.0, 6.0, ((0, 24), (1, 4), (2, 8)))
    doc_lengths = draw_doc_lengths(jax.random.fold_in(key_of[6], 71), 0)
    dest_index = draw_dest_index(jax.random.fold_in(key_of[6], 71), 0)
    return {"queries": queries, "key_rows": key_rows, "value_rows": value_rows, "grad_out": grad_out, "doc_lengths": doc_lengths, "dest_index": dest_index}


score_scale = 168.0 ** -0.5
neg_large = -1e30


def document_ids(lengths):
    boundary = jnp.cumsum(lengths, dtype=jnp.int32)
    positions = jnp.arange(LENGTH, dtype=jnp.int32)
    return jnp.sum((positions[:, None] >= boundary[None, :]).astype(jnp.int32), axis=1)


def sorted_order(dest_index):
    seq_count = dest_index.shape[0]
    blocked = dest_index.reshape(seq_count, LENGTH // ROWS, ROWS)
    ranking = blocked * ROWS + jnp.arange(ROWS, dtype=jnp.int32)
    return jnp.argsort(ranking, axis=-1).astype(jnp.int32)


def balance(whole, send_order):
    seq_count = whole.shape[0]
    span_count = LENGTH // ROWS
    group_rows = ROWS // seq_count
    col_count = whole.shape[2]
    blocks = whole.reshape(seq_count, span_count, ROWS, col_count)
    ranked = jnp.take_along_axis(blocks, send_order[..., None], axis=2)
    ranked = ranked.reshape(seq_count, span_count, seq_count, group_rows, col_count)
    return jnp.transpose(ranked, (2, 1, 0, 3, 4)).reshape(seq_count, LENGTH, col_count)


def unbalance(whole, send_order):
    seq_count = whole.shape[0]
    span_count = LENGTH // ROWS
    group_rows = ROWS // seq_count
    col_count = whole.shape[2]
    ranked = whole.reshape(seq_count, span_count, seq_count, group_rows, col_count)
    ranked = jnp.transpose(ranked, (2, 1, 0, 3, 4)).reshape(seq_count, span_count, ROWS, col_count)
    back_order = jnp.argsort(send_order, axis=-1).astype(jnp.int32)
    restored = jnp.take_along_axis(ranked, back_order[..., None], axis=2)
    return restored.reshape(seq_count, LENGTH, col_count)


def group_pass(query_two, key_one, value_one, grad_two, doc_ids):
    positions = jnp.arange(LENGTH, dtype=jnp.int32)
    key_wide = key_one.astype(jnp.float32)
    value_wide = value_one.astype(jnp.float32)

    def shard_step(carry, shard_index):
        key_acc, value_acc = carry
        start_row = shard_index * ROWS
        query_block = lax.dynamic_slice_in_dim(query_two, start_row, ROWS, 0).astype(jnp.float32)
        grad_block = lax.dynamic_slice_in_dim(grad_two, start_row, ROWS, 0).astype(jnp.float32)
        query_pos = start_row + jnp.arange(ROWS, dtype=jnp.int32)
        query_docs = lax.dynamic_slice_in_dim(doc_ids, start_row, ROWS, 0)
        distance = query_pos[:, None] - positions[None, :]
        allowed = (query_docs[:, None] == doc_ids[None, :]) & (distance >= 0) & (distance < WINDOW)
        scores = jnp.einsum("qhd,kd->hqk", query_block, key_wide) * score_scale
        scores = jnp.where(allowed[None], scores, neg_large)
        row_peak = jnp.max(scores, axis=2, keepdims=True)
        weights = jnp.where(allowed[None], jnp.exp(scores - row_peak), 0.0)
        prob_rows = weights / jnp.sum(weights, axis=2, keepdims=True)
        prob_low = lax.optimization_barrier(prob_rows.astype(jnp.bfloat16)).astype(jnp.float32)
        mixed_rows = jnp.einsum("hqk,kd->qhd", prob_low, value_wide).astype(jnp.bfloat16)
        value_part = jnp.einsum("hqk,qhd->kd", prob_low, grad_block)
        prob_grad = jnp.einsum("qhd,kd->hqk", grad_block, value_wide)
        center = jnp.sum(prob_rows * prob_grad, axis=2, keepdims=True)
        dscore = (prob_rows * (prob_grad - center) * score_scale).astype(jnp.bfloat16)
        dscore = lax.optimization_barrier(dscore).astype(jnp.float32)
        query_grad = jnp.einsum("hqk,kd->qhd", dscore, key_wide).astype(jnp.bfloat16)
        key_part = jnp.einsum("hqk,qhd->kd", dscore, query_block)
        key_low = lax.optimization_barrier(key_part.astype(jnp.bfloat16)).astype(jnp.float32)
        value_low = lax.optimization_barrier(value_part.astype(jnp.bfloat16)).astype(jnp.float32)
        return (key_acc + key_low, value_acc + value_low), (mixed_rows, query_grad)

    zero_rows = jnp.zeros((LENGTH, HEAD_DIM), jnp.float32)
    totals, blocks = lax.scan(shard_step, (zero_rows, zero_rows), jnp.arange(LENGTH // ROWS, dtype=jnp.int32))
    attended = blocks[0].reshape(LENGTH, 2, HEAD_DIM)
    query_grad = blocks[1].reshape(LENGTH, 2, HEAD_DIM)
    return attended, query_grad, totals[0].astype(jnp.bfloat16), totals[1].astype(jnp.bfloat16)


def one_sequence(inputs):
    query_seq, key_seq, value_seq, grad_seq, lengths = inputs
    doc_ids = document_ids(lengths)
    head_pairs = key_seq.shape[1] // HEAD_DIM
    query_split = jnp.transpose(query_seq.reshape(LENGTH, head_pairs, 2, HEAD_DIM), (1, 0, 2, 3))
    grad_split = jnp.transpose(grad_seq.reshape(LENGTH, head_pairs, 2, HEAD_DIM), (1, 0, 2, 3))
    key_split = jnp.transpose(key_seq.reshape(LENGTH, head_pairs, HEAD_DIM), (1, 0, 2))
    value_split = jnp.transpose(value_seq.reshape(LENGTH, head_pairs, HEAD_DIM), (1, 0, 2))

    def per_group(member):
        return group_pass(member[0], member[1], member[2], member[3], doc_ids)

    result = lax.map(per_group, (query_split, key_split, value_split, grad_split))
    attended = jnp.transpose(result[0], (1, 0, 2, 3)).reshape(LENGTH, head_pairs * 2 * HEAD_DIM)
    query_grad = jnp.transpose(result[1], (1, 0, 2, 3)).reshape(LENGTH, head_pairs * 2 * HEAD_DIM)
    key_grad = jnp.transpose(result[2], (1, 0, 2)).reshape(LENGTH, head_pairs * HEAD_DIM)
    value_grad = jnp.transpose(result[3], (1, 0, 2)).reshape(LENGTH, head_pairs * HEAD_DIM)
    return attended, query_grad, key_grad, value_grad


def reference(queries, key_rows, value_rows, grad_out, doc_lengths, dest_index):
    send_order = sorted_order(dest_index)
    query_bal = balance(queries, send_order)
    key_bal = balance(key_rows, send_order)
    value_bal = balance(value_rows, send_order)
    grad_bal = balance(grad_out, send_order)
    outcome = lax.map(one_sequence, (query_bal, key_bal, value_bal, grad_bal, doc_lengths))
    return (unbalance(outcome[0], send_order), unbalance(outcome[1], send_order), unbalance(outcome[2], send_order), unbalance(outcome[3], send_order))
```

```python
import functools
import math

import jax
import jax.numpy as jnp
from jax import lax
from jax.experimental import pallas as pl
from jax.experimental.pallas import tpu as pltpu
from jax.sharding import PartitionSpec as P

HEAD = 128
PAIR = 2 * HEAD
PAD = 16
WINDOW = 1024
DOCS = 4
SCALE = 168.0 ** (-0.5)
LOG2E = 1.0 / math.log(2.0)
NEG = -1e30
MESH = pl.DeviceIdType.MESH
BF16 = jnp.bfloat16
F32 = jnp.float32


def dot(a, b):
    return jnp.dot(a, b, preferred_element_type=F32)


def dot_nt(a, b):
    return lax.dot_general(a, b, (((1,), (1,)), ((), ())), preferred_element_type=F32)


def kernel(peers, spans, rows, window, *refs):
    (q_ref, k_ref, v_ref, dy_ref, len_ref, dest_ref, o_ref, dq_ref, dk_ref, dv_ref,
     xin, perm, unperm, sends, ctx, ctxt, recvs, homes, backs, gsend, grecv, acc,
     sbuf, dbuf, keyf, queryf, insem, ssem, rsem, xssem, xrsem) = refs
    me = lax.axis_index("dp")
    shard = lax.axis_index("seq")
    group = rows // peers
    padded = peers * PAD

    tail = padded - PAD * ((padded - rows + PAD - 1) // PAD)
    xin[pl.ds(tail, padded - tail), :] = jnp.zeros((padded - tail, 6 * HEAD), BF16)
    def fetch(ref, first, count, at, slot):
        return pltpu.make_async_copy(
            ref.at[0, :, pl.ds(first, count)],
            xin.at[pl.ds(0, rows), pl.ds(at, count)],
            insem.at[slot],
        )
    loads = [
        fetch(k_ref, 0, HEAD, 0, 0),
        fetch(v_ref, 0, HEAD, HEAD, 1),
        fetch(q_ref, 0, HEAD, 2 * HEAD, 2),
        fetch(dy_ref, 0, HEAD, 3 * HEAD, 3),
        fetch(q_ref, HEAD, HEAD, 4 * HEAD, 4),
        fetch(dy_ref, HEAD, HEAD, 5 * HEAD, 5),
    ]
    for load in loads:
        load.start()

    barrier = pltpu.get_barrier_semaphore()

    def greet(step, carry):
        pl.semaphore_signal(
            barrier, inc=1, device_id={"dp": lax.rem(me + step, peers)}, device_id_type=MESH
        )
        return carry

    lax.fori_loop(1, peers, greet, 0)
    for step in range(1, spans):
        pl.semaphore_signal(
            barrier, inc=1, device_id={"seq": lax.rem(shard + step, spans)}, device_id_type=MESH
        )

    dest = dest_ref[...]
    is_dest = (lax.broadcasted_iota(jnp.int32, (peers, rows), 0) == dest).astype(F32)
    before = (
        lax.broadcasted_iota(jnp.int32, (rows, rows), 0)
        < lax.broadcasted_iota(jnp.int32, (rows, rows), 1)
    ).astype(F32)
    counts = dot(is_dest.astype(BF16), before.astype(BF16))
    rank = jnp.sum(is_dest * counts, axis=0, keepdims=True)
    place = dest.astype(F32) * PAD + rank
    hot = (
        lax.broadcasted_iota(jnp.int32, (padded, rows), 0).astype(F32) == place
    ).astype(F32)
    perm[...] = jnp.zeros((padded, padded), F32)
    perm[:, pl.ds(0, rows)] = hot
    perm_low = perm[...].astype(BF16)

    def exchange(phase, src, dst):
        def one(step, carry):
            odd = lax.rem(step, 2)
            far = peers // 2 - (step + 1) // 2
            ahead = (1 - odd) * far + odd * (peers - far)
            peer = lax.rem(me + ahead, peers)
            pltpu.make_async_remote_copy(
                src_ref=src.at[pl.ds(pl.multiple_of(peer * PAD, PAD), PAD)],
                dst_ref=dst.at[pl.ds(pl.multiple_of(me * PAD, PAD), PAD)],
                send_sem=ssem.at[phase],
                recv_sem=rsem.at[phase],
                device_id={"dp": peer},
                device_id_type=MESH,
            ).start()
            return carry

        lax.fori_loop(0, peers - 1, one, 0)
        own = pl.ds(pl.multiple_of(me * PAD, PAD), PAD)
        pltpu.make_async_copy(src.at[own], dst.at[own], rsem.at[phase]).start()

    def arrived(phase, dst):
        pltpu.make_async_copy(dst, dst, rsem.at[phase]).wait()

    def departed(phase, src):
        sent = src.at[pl.ds(0, padded - PAD)]
        pltpu.make_async_copy(sent, sent, ssem.at[phase]).wait()

    landing = (ctx.at[pl.ds(0, padded)], recvs.at[0], recvs.at[1])
    for phase in range(3):
        loads[2 * phase].wait()
        loads[2 * phase + 1].wait()
        sends[phase] = dot(perm_low, xin[:, pl.ds(phase * PAIR, PAIR)]).astype(BF16)
        if phase == 0:
            pl.semaphore_wait(barrier, peers - 1 + spans - 1)
        exchange(phase, sends.at[phase], landing[phase])

    unperm[...] = perm[...].T.astype(BF16)
    bounds = [len_ref[0, 0]]
    for entry in range(1, DOCS):
        bounds.append(bounds[-1] + len_ref[0, entry])

    slot_row = lax.broadcasted_iota(jnp.int32, (padded, HEAD), 0)
    column = lax.broadcasted_iota(jnp.int32, (padded, HEAD), 1)
    local = (slot_row // PAD) * group + lax.rem(slot_row, PAD)
    blank = lax.rem(slot_row, PAD) >= group

    def documents(position):
        total = jnp.zeros_like(position)
        for bound in bounds:
            total = total + (position >= bound).astype(jnp.int32)
        return total

    queryf[...] = (documents(local + shard * rows) == column).astype(F32).astype(BF16)
    for back in range(spans):
        position = local + (shard - back) * rows
        shut = (documents(position) != column) | blank | (position < 0)
        keyf[pl.ds(back * padded, padded)] = jnp.where(
            shut & (column <= DOCS), NEG, 0.0
        ).astype(BF16)
    for back in range(1, spans):
        @pl.when(shard < back)
        def _():
            ctx[pl.ds(back * padded, padded)] = jnp.zeros((padded, PAIR), BF16)

    arrived(0, landing[0])

    def forward(back):
        return pltpu.make_async_remote_copy(
            src_ref=ctx.at[pl.ds(0, padded)],
            dst_ref=ctx.at[pl.ds(back * padded, padded)],
            send_sem=xssem.at[back],
            recv_sem=xrsem.at[back],
            device_id={"seq": lax.rem(shard + back, spans)},
            device_id_type=MESH,
        )

    for back in range(1, spans):
        @pl.when(shard + back < spans)
        def _():
            forward(back).start()
    for back in range(1, spans):
        @pl.when(shard >= back)
        def _():
            forward(back).wait_recv()
    for back in range(spans):
        block = pl.ds(back * padded, padded)
        ctxt[:, block] = ctx[block, :].astype(F32).T.astype(BF16)

    key_row = lax.broadcasted_iota(jnp.int32, (padded, padded), 0)
    query_col = lax.broadcasted_iota(jnp.int32, (padded, padded), 1)

    def spot(index):
        return (index // PAD) * group + lax.rem(index, PAD)

    def attend(member):
        arrived(1 + member, landing[1 + member])
        query = recvs[member, :, pl.ds(0, HEAD)]
        grad = recvs[member, :, pl.ds(HEAD, HEAD)]
        query_wide = jnp.concatenate([query, queryf[...]], axis=1)
        peak = None
        for back in range(spans):
            block = pl.ds(back * padded, padded)
            key_wide = jnp.concatenate([ctx[block, pl.ds(0, HEAD)], keyf[block, :]], axis=1)
            scores = dot_nt(key_wide, query_wide)
            if back == 0:
                scores = jnp.where(query_col >= key_row, scores, NEG)
            if back * rows + rows - 1 >= window:
                gap = back * rows + spot(query_col) - spot(key_row)
                scores = jnp.where(gap < window, scores, NEG)
            sbuf[block, :] = scores
            top = jnp.max(scores, axis=0, keepdims=True)
            peak = top if peak is None else jnp.maximum(peak, top)
        total = jnp.zeros((1, padded), F32)
        for back in range(spans):
            block = pl.ds(back * padded, padded)
            weight = jnp.exp2((sbuf[block, :] - peak) * (SCALE * LOG2E))
            sbuf[block, :] = weight
            total = total + jnp.sum(weight, axis=0, keepdims=True)
        share = 1.0 / total
        mixed = jnp.zeros((HEAD, padded), F32)
        center = jnp.zeros((1, padded), F32)
        for back in range(spans):
            block = pl.ds(back * padded, padded)
            prob = sbuf[block, :] * share
            sbuf[block, :] = prob
            low = prob.astype(BF16)
            dprob = dot_nt(ctx[block, pl.ds(HEAD, HEAD)], grad)
            dbuf[block, :] = dprob
            center = center + jnp.sum(prob * dprob, axis=0, keepdims=True)
            mixed = mixed + dot(ctxt[pl.ds(HEAD, HEAD), block], low)
            part = dot(low, grad)
            if member == 0:
                acc[block, pl.ds(HEAD, HEAD)] = part
            else:
                acc[block, pl.ds(HEAD, HEAD)] += part
        dquery = jnp.zeros((HEAD, padded), F32)
        for back in range(spans):
            block = pl.ds(back * padded, padded)
            dscore = (sbuf[block, :] * (dbuf[block, :] - center)).astype(BF16)
            dquery = dquery + dot(ctxt[pl.ds(0, HEAD), block], dscore)
            part = dot(dscore, query) * SCALE
            if member == 0:
                acc[block, pl.ds(0, HEAD)] = part
            else:
                acc[block, pl.ds(0, HEAD)] += part
        homes[member, :, pl.ds(0, HEAD)] = mixed.T.astype(BF16)
        homes[member, :, pl.ds(HEAD, HEAD)] = (dquery * SCALE).T.astype(BF16)
        exchange(3 + member, homes.at[member], backs.at[member])

    attend(0)
    attend(1)

    def give(back):
        return pltpu.make_async_remote_copy(
            src_ref=gsend.at[back],
            dst_ref=grecv.at[back],
            send_sem=xssem.at[spans + back],
            recv_sem=xrsem.at[spans + back],
            device_id={"seq": lax.rem(shard + spans - back, spans)},
            device_id_type=MESH,
        )

    for back in range(spans - 1, -1, -1):
        gsend[back] = acc[pl.ds(back * padded, padded), :].astype(BF16)
        if back > 0:
            @pl.when(shard >= back)
            def _():
                give(back).start()
    acc[pl.ds(0, padded), :] = gsend[0].astype(F32)
    for back in range(1, spans):
        @pl.when(shard + back < spans)
        def _():
            give(back).wait_recv()
            acc[pl.ds(0, padded), :] += grecv[back].astype(F32)
    homes[2] = acc[pl.ds(0, padded), :].astype(BF16)
    exchange(5, homes.at[2], backs.at[2])

    def settle(member):
        arrived(3 + member, backs.at[member])
        return dot(unperm[...], backs[member]).astype(BF16)

    for member in range(2):
        rows_home = settle(member)
        o_ref[0, :, pl.ds(member * HEAD, HEAD)] = rows_home[:rows, :HEAD]
        dq_ref[0, :, pl.ds(member * HEAD, HEAD)] = rows_home[:rows, HEAD:]
    rows_home = settle(2)
    dk_ref[0] = rows_home[:rows, :HEAD]
    dv_ref[0] = rows_home[:rows, HEAD:]

    for phase in range(3):
        departed(phase, sends.at[phase])
        departed(3 + phase, homes.at[phase])
    for back in range(1, spans):
        @pl.when(shard + back < spans)
        def _():
            forward(back).wait_send()
        @pl.when(shard >= back)
        def _():
            give(back).wait_send()


def solution(mesh, window=WINDOW):
    peers, spans = mesh.shape["dp"], mesh.shape["seq"]

    def local(queries, key_rows, value_rows, grad_out, doc_lengths, dest_index):
        rows = queries.shape[1]
        padded = peers * PAD
        blocks = spans * padded
        whole = pl.BlockSpec(memory_space=pltpu.VMEM)
        loose = pl.BlockSpec(memory_space=pl.ANY)
        return pl.pallas_call(
            functools.partial(kernel, peers, spans, rows, window),
            out_shape=(
                jax.ShapeDtypeStruct((1, rows, PAIR), BF16),
                jax.ShapeDtypeStruct((1, rows, PAIR), BF16),
                jax.ShapeDtypeStruct((1, rows, HEAD), BF16),
                jax.ShapeDtypeStruct((1, rows, HEAD), BF16),
            ),
            in_specs=[loose] * 4 + [pl.BlockSpec(memory_space=pltpu.SMEM), whole],
            out_specs=(whole,) * 4,
            scratch_shapes=[
                pltpu.VMEM((padded, 6 * HEAD), BF16),
                pltpu.VMEM((padded, padded), F32),
                pltpu.VMEM((padded, padded), BF16),
                pltpu.VMEM((3, padded, PAIR), BF16),
                pltpu.VMEM((blocks, PAIR), BF16),
                pltpu.VMEM((PAIR, blocks), BF16),
                pltpu.VMEM((2, padded, PAIR), BF16),
                pltpu.VMEM((3, padded, PAIR), BF16),
                pltpu.VMEM((3, padded, PAIR), BF16),
                pltpu.VMEM((spans, padded, PAIR), BF16),
                pltpu.VMEM((spans, padded, PAIR), BF16),
                pltpu.VMEM((blocks, PAIR), F32),
                pltpu.VMEM((blocks, padded), F32),
                pltpu.VMEM((blocks, padded), F32),
                pltpu.VMEM((blocks, HEAD), BF16),
                pltpu.VMEM((padded, HEAD), BF16),
                pltpu.SemaphoreType.DMA((6,)),
                pltpu.SemaphoreType.DMA((6,)),
                pltpu.SemaphoreType.DMA((6,)),
                pltpu.SemaphoreType.DMA((2 * spans,)),
                pltpu.SemaphoreType.DMA((2 * spans,)),
            ],
            compiler_params=pltpu.CompilerParams(
                collective_id=0, has_side_effects=True, vmem_limit_bytes=40 << 20
            ),
        )(queries, key_rows, value_rows, grad_out, doc_lengths, dest_index)

    wide = P("dp", "seq", "head")
    return jax.shard_map(
        local,
        mesh=mesh,
        in_specs=(wide, wide, wide, wide, P("dp", None), P("dp", "seq")),
        out_specs=(wide, wide, wide, wide),
        check_vma=False,
    )
```

```python
import functools
import math

import jax
import jax.numpy as jnp
from jax import lax
from jax.experimental import pallas as pl
from jax.experimental.pallas import tpu as pltpu
from jax.sharding import PartitionSpec as P

HEAD = 128
PAIR = 2 * HEAD
PAD = 16
WINDOW = 1024
DOCS = 4
SCALE = 168.0 ** (-0.5)
LOG2E = 1.0 / math.log(2.0)
NEG = -1e30
MESH = pl.DeviceIdType.MESH
BF16 = jnp.bfloat16
F32 = jnp.float32


def dot(a, b):
    return jnp.dot(a, b, preferred_element_type=F32)


def dot_nt(a, b):
    return lax.dot_general(a, b, (((1,), (1,)), ((), ())), preferred_element_type=F32)


def kernel(peers, spans, rows, window, *refs):
    (q_ref, k_ref, v_ref, dy_ref, len_ref, dest_ref, o_ref, dq_ref, dk_ref, dv_ref,
     lens, dests, xin, perm, unperm, sends, ctx, ctxt, recvs, homes, backs, gsend, grecv, acc,
     sbuf, dbuf, keyf, queryf, outs, insem, outsem, ssem, rsem, xssem, xrsem) = refs
    me = lax.axis_index("dp")
    shard = lax.axis_index("seq")
    group = rows // peers
    padded = peers * PAD

    dest_load = pltpu.make_async_copy(dest_ref, dests, insem.at[6])
    dest_load.start()

    tail = padded - PAD * ((padded - rows + PAD - 1) // PAD)
    xin[pl.ds(tail, padded - tail), :] = jnp.zeros((padded - tail, 6 * HEAD), BF16)
    def fetch(ref, first, count, at, slot):
        return pltpu.make_async_copy(
            ref.at[0, :, pl.ds(first, count)],
            xin.at[pl.ds(0, rows), pl.ds(at, count)],
            insem.at[slot],
        )
    loads = [
        fetch(k_ref, 0, HEAD, 0, 0),
        fetch(v_ref, 0, HEAD, HEAD, 1),
        fetch(q_ref, 0, HEAD, 2 * HEAD, 2),
        fetch(dy_ref, 0, HEAD, 3 * HEAD, 3),
        fetch(q_ref, HEAD, HEAD, 4 * HEAD, 4),
        fetch(dy_ref, HEAD, HEAD, 5 * HEAD, 5),
    ]
    for load in loads:
        load.start()
    lens_load = pltpu.make_async_copy(len_ref, lens, insem.at[7])
    lens_load.start()

    barrier = pltpu.get_barrier_semaphore()

    def greet(step, carry):
        pl.semaphore_signal(
            barrier, inc=1, device_id={"dp": lax.rem(me + step, peers)}, device_id_type=MESH
        )
        return carry

    lax.fori_loop(1, peers, greet, 0)
    for step in range(1, spans):
        pl.semaphore_signal(
            barrier, inc=1, device_id={"seq": lax.rem(shard + step, spans)}, device_id_type=MESH
        )

    dest_load.wait()
    dest = dests[...]
    is_dest = (lax.broadcasted_iota(jnp.int32, (peers, rows), 0) == dest).astype(F32)
    before = (
        lax.broadcasted_iota(jnp.int32, (rows, rows), 0)
        < lax.broadcasted_iota(jnp.int32, (rows, rows), 1)
    ).astype(F32)
    counts = dot(is_dest.astype(BF16), before.astype(BF16))
    rank = jnp.sum(is_dest * counts, axis=0, keepdims=True)
    place = dest.astype(F32) * PAD + rank
    hot = (
        lax.broadcasted_iota(jnp.int32, (padded, rows), 0).astype(F32) == place
    ).astype(F32)
    perm[...] = jnp.zeros((padded, padded), F32)
    perm[:, pl.ds(0, rows)] = hot
    perm_low = perm[...].astype(BF16)

    def exchange(phase, src, dst):
        def one(step, carry):
            odd = lax.rem(step, 2)
            far = peers // 2 - (step + 1) // 2
            ahead = (1 - odd) * far + odd * (peers - far)
            peer = lax.rem(me + ahead, peers)
            pltpu.make_async_remote_copy(
                src_ref=src.at[pl.ds(pl.multiple_of(peer * PAD, PAD), PAD)],
                dst_ref=dst.at[pl.ds(pl.multiple_of(me * PAD, PAD), PAD)],
                send_sem=ssem.at[phase],
                recv_sem=rsem.at[phase],
                device_id={"dp": peer},
                device_id_type=MESH,
            ).start()
            return carry

        lax.fori_loop(0, peers - 1, one, 0)
        own = pl.ds(pl.multiple_of(me * PAD, PAD), PAD)
        pltpu.make_async_copy(src.at[own], dst.at[own], rsem.at[phase]).start()

    def arrived(phase, dst):
        pltpu.make_async_copy(dst, dst, rsem.at[phase]).wait()

    def departed(phase, src):
        sent = src.at[pl.ds(0, padded - PAD)]
        pltpu.make_async_copy(sent, sent, ssem.at[phase]).wait()

    landing = (ctx.at[pl.ds(0, padded)], recvs.at[0], recvs.at[1])
    for phase in range(3):
        loads[2 * phase].wait()
        loads[2 * phase + 1].wait()
        sends[phase] = dot(perm_low, xin[:, pl.ds(phase * PAIR, PAIR)]).astype(BF16)
        if phase == 0:
            pl.semaphore_wait(barrier, peers - 1 + spans - 1)
        exchange(phase, sends.at[phase], landing[phase])

    unperm[...] = perm[...].T.astype(BF16)
    lens_load.wait()
    bounds = [lens[0, 0]]
    for entry in range(1, DOCS):
        bounds.append(bounds[-1] + lens[0, entry])

    slot_row = lax.broadcasted_iota(jnp.int32, (padded, HEAD), 0)
    column = lax.broadcasted_iota(jnp.int32, (padded, HEAD), 1)
    local = (slot_row // PAD) * group + lax.rem(slot_row, PAD)
    blank = lax.rem(slot_row, PAD) >= group

    def documents(position):
        total = jnp.zeros_like(position)
        for bound in bounds:
            total = total + (position >= bound).astype(jnp.int32)
        return total

    queryf[...] = (documents(local + shard * rows) == column).astype(F32).astype(BF16)
    for back in range(spans):
        position = local + (shard - back) * rows
        shut = (documents(position) != column) | blank | (position < 0)
        keyf[pl.ds(back * padded, padded)] = jnp.where(
            shut & (column <= DOCS), NEG, 0.0
        ).astype(BF16)
    for back in range(1, spans):
        @pl.when(shard < back)
        def _():
            ctx[pl.ds(back * padded, padded)] = jnp.zeros((padded, PAIR), BF16)

    arrived(0, landing[0])

    def forward(back):
        near = back < spans - 1
        return pltpu.make_async_remote_copy(
            src_ref=ctx.at[pl.ds((back - 1 if near else 0) * padded, padded)],
            dst_ref=ctx.at[pl.ds(back * padded, padded)],
            send_sem=xssem.at[back],
            recv_sem=xrsem.at[back],
            device_id={"seq": lax.rem(shard + (1 if near else back), spans)},
            device_id_type=MESH,
        )

    def forwards(back):
        if back < spans - 1:
            return (shard >= back - 1) & (shard + 1 < spans)
        return shard + back < spans

    def pass_on(back):
        @pl.when(forwards(back))
        def _():
            forward(back).start()

    def take(back):
        @pl.when(shard >= back)
        def _():
            forward(back).wait_recv()

    pass_on(1)
    pass_on(spans - 1)
    for back in range(1, spans - 1):
        take(back)
        if back + 1 < spans - 1:
            pass_on(back + 1)
    take(spans - 1)
    for back in range(spans):
        block = pl.ds(back * padded, padded)
        ctxt[:, block] = ctx[block, :].astype(F32).T.astype(BF16)

    key_row = lax.broadcasted_iota(jnp.int32, (padded, padded), 0)
    query_col = lax.broadcasted_iota(jnp.int32, (padded, padded), 1)

    def spot(index):
        return (index // PAD) * group + lax.rem(index, PAD)

    def attend(member):
        arrived(1 + member, landing[1 + member])
        query = recvs[member, :, pl.ds(0, HEAD)]
        grad = recvs[member, :, pl.ds(HEAD, HEAD)]
        query_wide = jnp.concatenate([query, queryf[...]], axis=1)
        peak = None
        for back in range(spans):
            block = pl.ds(back * padded, padded)
            key_wide = jnp.concatenate([ctx[block, pl.ds(0, HEAD)], keyf[block, :]], axis=1)
            scores = dot_nt(key_wide, query_wide)
            if back == 0:
                scores = jnp.where(query_col >= key_row, scores, NEG)
            if back * rows + rows - 1 >= window:
                gap = back * rows + spot(query_col) - spot(key_row)
                scores = jnp.where(gap < window, scores, NEG)
            sbuf[block, :] = scores
            top = jnp.max(scores, axis=0, keepdims=True)
            peak = top if peak is None else jnp.maximum(peak, top)
        total = jnp.zeros((1, padded), F32)
        for back in range(spans):
            block = pl.ds(back * padded, padded)
            weight = jnp.exp2((sbuf[block, :] - peak) * (SCALE * LOG2E))
            sbuf[block, :] = weight
            total = total + jnp.sum(weight, axis=0, keepdims=True)
        share = 1.0 / total
        mixed = jnp.zeros((HEAD, padded), F32)
        center = jnp.zeros((1, padded), F32)
        for back in range(spans):
            block = pl.ds(back * padded, padded)
            prob = sbuf[block, :] * share
            sbuf[block, :] = prob
            low = prob.astype(BF16)
            dprob = dot_nt(ctx[block, pl.ds(HEAD, HEAD)], grad)
            dbuf[block, :] = dprob
            center = center + jnp.sum(prob * dprob, axis=0, keepdims=True)
            mixed = mixed + dot(ctxt[pl.ds(HEAD, HEAD), block], low)
            part = dot(low, grad)
            if member == 0:
                acc[block, pl.ds(HEAD, HEAD)] = part
            else:
                acc[block, pl.ds(HEAD, HEAD)] += part
        dquery = jnp.zeros((HEAD, padded), F32)
        for back in range(spans):
            block = pl.ds(back * padded, padded)
            dscore = (sbuf[block, :] * (dbuf[block, :] - center)).astype(BF16)
            dquery = dquery + dot(ctxt[pl.ds(0, HEAD), block], dscore)
            part = dot(dscore, query) * SCALE
            if member == 0:
                acc[block, pl.ds(0, HEAD)] = part
            else:
                acc[block, pl.ds(0, HEAD)] += part
        homes[member, :, pl.ds(0, HEAD)] = mixed.T.astype(BF16)
        homes[member, :, pl.ds(HEAD, HEAD)] = (dquery * SCALE).T.astype(BF16)
        exchange(3 + member, homes.at[member], backs.at[member])

    attend(0)
    attend(1)

    def give(back):
        near = back < spans - 1
        return pltpu.make_async_remote_copy(
            src_ref=gsend.at[back],
            dst_ref=grecv.at[back],
            send_sem=xssem.at[spans + back],
            recv_sem=xrsem.at[spans + back],
            device_id={"seq": lax.rem(shard + spans - (1 if near else back), spans)},
            device_id_type=MESH,
        )

    def gets(back):
        if back < spans - 1:
            return (shard + 1 < spans) & (shard + 1 >= back)
        return shard + back < spans

    for back in range(spans - 1, -1, -1):
        gsend[back] = acc[pl.ds(back * padded, padded), :].astype(BF16)
        if 0 < back < spans - 2:
            @pl.when(gets(back + 1))
            def _():
                give(back + 1).wait_recv()
                gsend[back] = (gsend[back].astype(F32) + grecv[back + 1].astype(F32)).astype(BF16)
        if back > 0:
            @pl.when(shard >= back)
            def _():
                give(back).start()
    acc[pl.ds(0, padded), :] = gsend[0].astype(F32)
    for back in (spans - 1, 1):
        @pl.when(gets(back))
        def _():
            give(back).wait_recv()
            acc[pl.ds(0, padded), :] += grecv[back].astype(F32)
    homes[2] = acc[pl.ds(0, padded), :].astype(BF16)
    exchange(5, homes.at[2], backs.at[2])

    homeward = []

    def settle(member, first, second, at):
        arrived(3 + member, backs.at[member])
        outs[member] = dot(unperm[...], backs[member]).astype(BF16)
        for half, out in enumerate((first, second)):
            store = pltpu.make_async_copy(
                outs.at[member, pl.ds(0, rows), pl.ds(half * HEAD, HEAD)],
                out.at[0, :, pl.ds(at, HEAD)],
                outsem.at[2 * member + half],
            )
            store.start()
            homeward.append(store)

    settle(0, o_ref, dq_ref, 0)
    settle(1, o_ref, dq_ref, HEAD)
    settle(2, dk_ref, dv_ref, 0)

    for phase in range(3):
        departed(phase, sends.at[phase])
        departed(3 + phase, homes.at[phase])
    for back in range(1, spans):
        @pl.when(forwards(back))
        def _():
            forward(back).wait_send()
        @pl.when(shard >= back)
        def _():
            give(back).wait_send()
    for store in homeward:
        store.wait()


def deliver(*refs):
    sources, targets, sem = refs[:4], refs[4:8], refs[8]
    copies = [
        pltpu.make_async_copy(source, target, sem.at[at])
        for at, (source, target) in enumerate(zip(sources, targets))
    ]
    for copy in copies:
        copy.start()
    for copy in copies:
        copy.wait()


def solution(mesh, window=WINDOW):
    peers, spans = mesh.shape["dp"], mesh.shape["seq"]

    def local(queries, key_rows, value_rows, grad_out, doc_lengths, dest_index):
        rows = queries.shape[1]
        padded = peers * PAD
        blocks = spans * padded
        loose = pl.BlockSpec(memory_space=pl.ANY)
        shapes = tuple(
            jax.ShapeDtypeStruct((1, rows, columns), BF16) for columns in (PAIR, PAIR, HEAD, HEAD)
        )
        landed = pl.pallas_call(
            functools.partial(kernel, peers, spans, rows, window),
            out_shape=shapes,
            in_specs=[loose] * 6,
            out_specs=(loose,) * 4,
            scratch_shapes=[
                pltpu.SMEM((1, DOCS), jnp.int32),
                pltpu.VMEM((1, rows), jnp.int32),
                pltpu.VMEM((padded, 6 * HEAD), BF16),
                pltpu.VMEM((padded, padded), F32),
                pltpu.VMEM((padded, padded), BF16),
                pltpu.VMEM((3, padded, PAIR), BF16),
                pltpu.VMEM((blocks, PAIR), BF16),
                pltpu.VMEM((PAIR, blocks), BF16),
                pltpu.VMEM((2, padded, PAIR), BF16),
                pltpu.VMEM((3, padded, PAIR), BF16),
                pltpu.VMEM((3, padded, PAIR), BF16),
                pltpu.VMEM((spans, padded, PAIR), BF16),
                pltpu.VMEM((spans, padded, PAIR), BF16),
                pltpu.VMEM((blocks, PAIR), F32),
                pltpu.VMEM((blocks, padded), F32),
                pltpu.VMEM((blocks, padded), F32),
                pltpu.VMEM((blocks, HEAD), BF16),
                pltpu.VMEM((padded, HEAD), BF16),
                pltpu.VMEM((3, padded, PAIR), BF16),
                pltpu.SemaphoreType.DMA((8,)),
                pltpu.SemaphoreType.DMA((6,)),
                pltpu.SemaphoreType.DMA((6,)),
                pltpu.SemaphoreType.DMA((6,)),
                pltpu.SemaphoreType.DMA((2 * spans,)),
                pltpu.SemaphoreType.DMA((2 * spans,)),
            ],
            compiler_params=pltpu.CompilerParams(
                collective_id=0, has_side_effects=True, vmem_limit_bytes=60 << 20
            ),
        )(queries, key_rows, value_rows, grad_out, doc_lengths, dest_index)
        return pl.pallas_call(
            deliver,
            out_shape=shapes,
            in_specs=[loose] * 4,
            out_specs=(loose,) * 4,
            scratch_shapes=[pltpu.SemaphoreType.DMA((4,))],
        )(*landed)

    wide = P("dp", "seq", "head")
    return jax.shard_map(
        local,
        mesh=mesh,
        in_specs=(wide, wide, wide, wide, P("dp", None), P("dp", "seq")),
        out_specs=(wide, wide, wide, wide),
        check_vma=False,
    )
```

```python
import functools
import math

import jax
import jax.numpy as jnp
from jax import lax
from jax.experimental import pallas as pl
from jax.experimental.pallas import tpu as pltpu
from jax.sharding import PartitionSpec as P

HEAD = 128
PAIR = 2 * HEAD
PAD = 16
WINDOW = 1024
DOCS = 4
SCALE = 168.0 ** (-0.5)
LOG2E = 1.0 / math.log(2.0)
NEG = -1e30
MESH = pl.DeviceIdType.MESH
BF16 = jnp.bfloat16
F32 = jnp.float32


def dot(a, b):
    return jnp.dot(a, b, preferred_element_type=F32)


def dot_nt(a, b):
    return lax.dot_general(a, b, (((1,), (1,)), ((), ())), preferred_element_type=F32)


def kernel(peers, spans, rows, window, *refs):
    (q_ref, k_ref, v_ref, dy_ref, len_ref, dest_ref, o_ref, dq_ref, dk_ref, dv_ref,
     lens, dests, xin, perm, unperm, sends, ctx, ctxt, recvs, homes, backs, gsend, grecv, acc,
     sbuf, dbuf, keyf, queryf, outs, insem, outsem, ssem, rsem, xssem, xrsem) = refs
    me = lax.axis_index("dp")
    shard = lax.axis_index("seq")
    group = rows // peers
    padded = peers * PAD

    dest_load = pltpu.make_async_copy(dest_ref, dests, insem.at[6])
    dest_load.start()

    tail = padded - PAD * ((padded - rows + PAD - 1) // PAD)
    xin[pl.ds(tail, padded - tail), :] = jnp.zeros((padded - tail, 6 * HEAD), BF16)
    def fetch(ref, first, count, at, slot):
        return pltpu.make_async_copy(
            ref.at[0, :, pl.ds(first, count)],
            xin.at[pl.ds(0, rows), pl.ds(at, count)],
            insem.at[slot],
        )
    loads = [
        fetch(k_ref, 0, HEAD, 0, 0),
        fetch(v_ref, 0, HEAD, HEAD, 1),
        fetch(q_ref, 0, HEAD, 2 * HEAD, 2),
        fetch(dy_ref, 0, HEAD, 3 * HEAD, 3),
        fetch(q_ref, HEAD, HEAD, 4 * HEAD, 4),
        fetch(dy_ref, HEAD, HEAD, 5 * HEAD, 5),
    ]
    for load in loads:
        load.start()
    lens_load = pltpu.make_async_copy(len_ref, lens, insem.at[7])
    lens_load.start()

    barrier = pltpu.get_barrier_semaphore()

    def greet(step, carry):
        pl.semaphore_signal(
            barrier, inc=1, device_id={"dp": lax.rem(me + step, peers)}, device_id_type=MESH
        )
        return carry

    lax.fori_loop(1, peers, greet, 0)
    for step in range(1, spans):
        pl.semaphore_signal(
            barrier, inc=1, device_id={"seq": lax.rem(shard + step, spans)}, device_id_type=MESH
        )

    dest_load.wait()
    dest = dests[...]
    is_dest = (lax.broadcasted_iota(jnp.int32, (peers, rows), 0) == dest).astype(F32)
    before = (
        lax.broadcasted_iota(jnp.int32, (rows, rows), 0)
        < lax.broadcasted_iota(jnp.int32, (rows, rows), 1)
    ).astype(F32)
    counts = dot(is_dest.astype(BF16), before.astype(BF16))
    rank = jnp.sum(is_dest * counts, axis=0, keepdims=True)
    place = dest.astype(F32) * PAD + rank
    hot = (
        lax.broadcasted_iota(jnp.int32, (padded, rows), 0).astype(F32) == place
    ).astype(F32)
    perm[...] = jnp.zeros((padded, padded), F32)
    perm[:, pl.ds(0, rows)] = hot
    perm_low = perm[...].astype(BF16)

    def exchange(phase, src, dst):
        def one(step, carry):
            odd = lax.rem(step, 2)
            far = peers // 2 - (step + 1) // 2
            ahead = (1 - odd) * far + odd * (peers - far)
            peer = lax.rem(me + ahead, peers)
            pltpu.make_async_remote_copy(
                src_ref=src.at[pl.ds(pl.multiple_of(peer * PAD, PAD), PAD)],
                dst_ref=dst.at[pl.ds(pl.multiple_of(me * PAD, PAD), PAD)],
                send_sem=ssem.at[phase],
                recv_sem=rsem.at[phase],
                device_id={"dp": peer},
                device_id_type=MESH,
            ).start()
            return carry

        lax.fori_loop(0, peers - 1, one, 0)
        own = pl.ds(pl.multiple_of(me * PAD, PAD), PAD)
        pltpu.make_async_copy(src.at[own], dst.at[own], rsem.at[phase]).start()

    def arrived(phase, dst):
        pltpu.make_async_copy(dst, dst, rsem.at[phase]).wait()

    def departed(phase, src):
        sent = src.at[pl.ds(0, padded - PAD)]
        pltpu.make_async_copy(sent, sent, ssem.at[phase]).wait()

    landing = (ctx.at[pl.ds(0, padded)], recvs.at[0], recvs.at[1])
    for phase in range(3):
        loads[2 * phase].wait()
        loads[2 * phase + 1].wait()
        sends[phase] = dot(perm_low, xin[:, pl.ds(phase * PAIR, PAIR)]).astype(BF16)
        if phase == 0:
            pl.semaphore_wait(barrier, peers - 1 + spans - 1)
        exchange(phase, sends.at[phase], landing[phase])

    unperm[...] = perm[...].T.astype(BF16)
    lens_load.wait()
    bounds = [lens[0, 0]]
    for entry in range(1, DOCS):
        bounds.append(bounds[-1] + lens[0, entry])

    slot_row = lax.broadcasted_iota(jnp.int32, (padded, HEAD), 0)
    column = lax.broadcasted_iota(jnp.int32, (padded, HEAD), 1)
    local = (slot_row // PAD) * group + lax.rem(slot_row, PAD)
    blank = lax.rem(slot_row, PAD) >= group

    def documents(position):
        total = jnp.zeros_like(position)
        for bound in bounds:
            total = total + (position >= bound).astype(jnp.int32)
        return total

    queryf[...] = (documents(local + shard * rows) == column).astype(F32).astype(BF16)
    for back in range(spans):
        position = local + (shard - back) * rows
        shut = (documents(position) != column) | blank | (position < 0)
        keyf[pl.ds(back * padded, padded)] = jnp.where(
            shut & (column <= DOCS), NEG, 0.0
        ).astype(BF16)
    for back in range(1, spans):
        @pl.when(shard < back)
        def _():
            ctx[pl.ds(back * padded, padded)] = jnp.zeros((padded, PAIR), BF16)

    arrived(0, landing[0])

    def forward(back):
        near = back < spans - 1
        return pltpu.make_async_remote_copy(
            src_ref=ctx.at[pl.ds((back - 1 if near else 0) * padded, padded)],
            dst_ref=ctx.at[pl.ds(back * padded, padded)],
            send_sem=xssem.at[back],
            recv_sem=xrsem.at[back],
            device_id={"seq": lax.rem(shard + (1 if near else back), spans)},
            device_id_type=MESH,
        )

    def forwards(back):
        if back < spans - 1:
            return (shard >= back - 1) & (shard + 1 < spans)
        return shard + back < spans

    def pass_on(back):
        @pl.when(forwards(back))
        def _():
            forward(back).start()

    def take(back):
        @pl.when(shard >= back)
        def _():
            forward(back).wait_recv()

    pass_on(1)
    pass_on(spans - 1)
    for back in range(1, spans - 1):
        take(back)
        if back + 1 < spans - 1:
            pass_on(back + 1)
    take(spans - 1)
    for back in range(spans):
        block = pl.ds(back * padded, padded)
        ctxt[:, block] = ctx[block, :].astype(F32).T.astype(BF16)

    key_row = lax.broadcasted_iota(jnp.int32, (padded, padded), 0)
    query_col = lax.broadcasted_iota(jnp.int32, (padded, padded), 1)

    def spot(index):
        return (index // PAD) * group + lax.rem(index, PAD)

    def attend(member):
        arrived(1 + member, landing[1 + member])
        query = recvs[member, :, pl.ds(0, HEAD)]
        grad = recvs[member, :, pl.ds(HEAD, HEAD)]
        query_wide = jnp.concatenate([query, queryf[...]], axis=1)
        peak = None
        for back in range(spans):
            block = pl.ds(back * padded, padded)
            key_wide = jnp.concatenate([ctx[block, pl.ds(0, HEAD)], keyf[block, :]], axis=1)
            scores = dot_nt(key_wide, query_wide)
            if back == 0:
                scores = jnp.where(query_col >= key_row, scores, NEG)
            if back * rows + rows - 1 >= window:
                gap = back * rows + spot(query_col) - spot(key_row)
                scores = jnp.where(gap < window, scores, NEG)
            sbuf[block, :] = scores
            top = jnp.max(scores, axis=0, keepdims=True)
            peak = top if peak is None else jnp.maximum(peak, top)
        total = jnp.zeros((1, padded), F32)
        for back in range(spans):
            block = pl.ds(back * padded, padded)
            weight = jnp.exp2((sbuf[block, :] - peak) * (SCALE * LOG2E))
            sbuf[block, :] = weight
            total = total + jnp.sum(weight, axis=0, keepdims=True)
        share = 1.0 / total
        mixed = jnp.zeros((HEAD, padded), F32)
        center = jnp.zeros((1, padded), F32)
        for back in range(spans):
            block = pl.ds(back * padded, padded)
            prob = sbuf[block, :] * share
            sbuf[block, :] = prob
            low = prob.astype(BF16)
            dprob = dot_nt(ctx[block, pl.ds(HEAD, HEAD)], grad)
            dbuf[block, :] = dprob
            center = center + jnp.sum(prob * dprob, axis=0, keepdims=True)
            mixed = mixed + dot(ctxt[pl.ds(HEAD, HEAD), block], low)
            part = dot(low, grad)
            if member == 0:
                acc[block, pl.ds(HEAD, HEAD)] = part
            else:
                acc[block, pl.ds(HEAD, HEAD)] += part
        dquery = jnp.zeros((HEAD, padded), F32)
        for back in range(spans):
            block = pl.ds(back * padded, padded)
            dscore = (sbuf[block, :] * (dbuf[block, :] - center)).astype(BF16)
            dquery = dquery + dot(ctxt[pl.ds(0, HEAD), block], dscore)
            part = dot(dscore, query) * SCALE
            if member == 0:
                acc[block, pl.ds(0, HEAD)] = part
            else:
                acc[block, pl.ds(0, HEAD)] += part
        homes[member, :, pl.ds(0, HEAD)] = mixed.T.astype(BF16)
        homes[member, :, pl.ds(HEAD, HEAD)] = (dquery * SCALE).T.astype(BF16)
        exchange(3 + member, homes.at[member], backs.at[member])

    attend(0)
    attend(1)

    def give(back):
        near = back < spans - 1
        return pltpu.make_async_remote_copy(
            src_ref=gsend.at[back],
            dst_ref=grecv.at[back],
            send_sem=xssem.at[spans + back],
            recv_sem=xrsem.at[spans + back],
            device_id={"seq": lax.rem(shard + spans - (1 if near else back), spans)},
            device_id_type=MESH,
        )

    def gets(back):
        if back < spans - 1:
            return (shard + 1 < spans) & (shard + 1 >= back)
        return shard + back < spans

    for back in range(spans - 1, -1, -1):
        gsend[back] = acc[pl.ds(back * padded, padded), :].astype(BF16)
        if 0 < back < spans - 2:
            @pl.when(gets(back + 1))
            def _():
                give(back + 1).wait_recv()
                gsend[back] = (gsend[back].astype(F32) + grecv[back + 1].astype(F32)).astype(BF16)
        if back > 0:
            @pl.when(shard >= back)
            def _():
                give(back).start()
    acc[pl.ds(0, padded), :] = gsend[0].astype(F32)
    for back in (spans - 1, 1):
        @pl.when(gets(back))
        def _():
            give(back).wait_recv()
            acc[pl.ds(0, padded), :] += grecv[back].astype(F32)
    homes[2] = acc[pl.ds(0, padded), :].astype(BF16)
    exchange(5, homes.at[2], backs.at[2])

    homeward = []

    def settle(member, first, second, at):
        arrived(3 + member, backs.at[member])
        outs[member] = dot(unperm[...], backs[member]).astype(BF16)
        for half, out in enumerate((first, second)):
            store = pltpu.make_async_copy(
                outs.at[member, pl.ds(0, rows), pl.ds(half * HEAD, HEAD)],
                out.at[0, :, pl.ds(at, HEAD)],
                outsem.at[2 * member + half],
            )
            store.start()
            homeward.append(store)

    settle(0, o_ref, dq_ref, 0)
    settle(1, o_ref, dq_ref, HEAD)
    settle(2, dk_ref, dv_ref, 0)

    for phase in range(3):
        departed(phase, sends.at[phase])
        departed(3 + phase, homes.at[phase])
    for back in range(1, spans):
        @pl.when(forwards(back))
        def _():
            forward(back).wait_send()
        @pl.when(shard >= back)
        def _():
            give(back).wait_send()
    for store in homeward:
        store.wait()


def deliver(*refs):
    sources, targets, holds = refs[:4], refs[4:8], refs[8:12]
    insem, outsem = refs[12:]
    loads = [
        pltpu.make_async_copy(source, hold, insem.at[at])
        for at, (source, hold) in enumerate(zip(sources, holds))
    ]
    stores = [
        pltpu.make_async_copy(hold, target, outsem.at[at])
        for at, (hold, target) in enumerate(zip(holds, targets))
    ]
    for load in loads:
        load.start()
    for load, store in zip(loads, stores):
        load.wait()
        store.start()
    for store in stores:
        store.wait()


def solution(mesh, window=WINDOW):
    peers, spans = mesh.shape["dp"], mesh.shape["seq"]

    def local(queries, key_rows, value_rows, grad_out, doc_lengths, dest_index):
        rows = queries.shape[1]
        padded = peers * PAD
        blocks = spans * padded
        loose = pl.BlockSpec(memory_space=pl.ANY)
        shapes = tuple(
            jax.ShapeDtypeStruct((1, rows, columns), BF16) for columns in (PAIR, PAIR, HEAD, HEAD)
        )
        landed = pl.pallas_call(
            functools.partial(kernel, peers, spans, rows, window),
            out_shape=shapes,
            in_specs=[loose] * 6,
            out_specs=(loose,) * 4,
            scratch_shapes=[
                pltpu.SMEM((1, DOCS), jnp.int32),
                pltpu.VMEM((1, rows), jnp.int32),
                pltpu.VMEM((padded, 6 * HEAD), BF16),
                pltpu.VMEM((padded, padded), F32),
                pltpu.VMEM((padded, padded), BF16),
                pltpu.VMEM((3, padded, PAIR), BF16),
                pltpu.VMEM((blocks, PAIR), BF16),
                pltpu.VMEM((PAIR, blocks), BF16),
                pltpu.VMEM((2, padded, PAIR), BF16),
                pltpu.VMEM((3, padded, PAIR), BF16),
                pltpu.VMEM((3, padded, PAIR), BF16),
                pltpu.VMEM((spans, padded, PAIR), BF16),
                pltpu.VMEM((spans, padded, PAIR), BF16),
                pltpu.VMEM((blocks, PAIR), F32),
                pltpu.VMEM((blocks, padded), F32),
                pltpu.VMEM((blocks, padded), F32),
                pltpu.VMEM((blocks, HEAD), BF16),
                pltpu.VMEM((padded, HEAD), BF16),
                pltpu.VMEM((3, padded, PAIR), BF16),
                pltpu.SemaphoreType.DMA((8,)),
                pltpu.SemaphoreType.DMA((6,)),
                pltpu.SemaphoreType.DMA((6,)),
                pltpu.SemaphoreType.DMA((6,)),
                pltpu.SemaphoreType.DMA((2 * spans,)),
                pltpu.SemaphoreType.DMA((2 * spans,)),
            ],
            compiler_params=pltpu.CompilerParams(
                collective_id=0, has_side_effects=True, vmem_limit_bytes=60 << 20
            ),
        )(queries, key_rows, value_rows, grad_out, doc_lengths, dest_index)
        return pl.pallas_call(
            deliver,
            out_shape=shapes,
            in_specs=[loose] * 4,
            out_specs=(loose,) * 4,
            scratch_shapes=[
                *(pltpu.VMEM(shape.shape, BF16) for shape in shapes),
                pltpu.SemaphoreType.DMA((4,)),
                pltpu.SemaphoreType.DMA((4,)),
            ],
        )(*landed)

    wide = P("dp", "seq", "head")
    return jax.shard_map(
        local,
        mesh=mesh,
        in_specs=(wide, wide, wide, wide, P("dp", None), P("dp", "seq")),
        out_specs=(wide, wide, wide, wide),
        check_vma=False,
    )
```

```python
import functools
import math

import jax
import jax.numpy as jnp
from jax import lax
from jax.experimental import pallas as pl
from jax.experimental.pallas import tpu as pltpu
from jax.sharding import PartitionSpec as P

HEAD = 128
PAIR = 2 * HEAD
PAD = 16
WINDOW = 1024
DOCS = 4
SCALE = 168.0 ** (-0.5)
LOG2E = 1.0 / math.log(2.0)
NEG = -1e30
MESH = pl.DeviceIdType.MESH
BF16 = jnp.bfloat16
F32 = jnp.float32


def dot(a, b):
    return jnp.dot(a, b, preferred_element_type=F32)


def dot_nt(a, b):
    return lax.dot_general(a, b, (((1,), (1,)), ((), ())), preferred_element_type=F32)


def kernel(peers, spans, rows, window, *refs):
    (q_ref, k_ref, v_ref, dy_ref, len_ref, dest_ref, o_ref, dq_ref, dk_ref, dv_ref,
     lens, dests, xin, perm, unperm, sends, ctx, ctxt, recvs, homes, backs, gsend, grecv, acc,
     sbuf, dbuf, gaps, keyf, queryf, outs, insem, outsem, ssem, rsem, xssem, xrsem) = refs
    me = lax.axis_index("dp")
    shard = lax.axis_index("seq")
    group = rows // peers
    padded = peers * PAD
    pieces = peers // 2

    dest_load = pltpu.make_async_copy(dest_ref, dests, insem.at[6])
    dest_load.start()

    tail = padded - PAD * ((padded - rows + PAD - 1) // PAD)
    xin[pl.ds(tail, padded - tail), :] = jnp.zeros((padded - tail, 6 * HEAD), BF16)
    def fetch(ref, first, count, at, slot):
        return pltpu.make_async_copy(
            ref.at[0, :, pl.ds(first, count)],
            xin.at[pl.ds(0, rows), pl.ds(at, count)],
            insem.at[slot],
        )
    loads = [
        fetch(k_ref, 0, HEAD, 0, 0),
        fetch(v_ref, 0, HEAD, HEAD, 1),
        fetch(q_ref, 0, HEAD, 2 * HEAD, 2),
        fetch(dy_ref, 0, HEAD, 3 * HEAD, 3),
        fetch(q_ref, HEAD, HEAD, 4 * HEAD, 4),
        fetch(dy_ref, HEAD, HEAD, 5 * HEAD, 5),
    ]
    for load in loads:
        load.start()
    lens_load = pltpu.make_async_copy(len_ref, lens, insem.at[7])
    lens_load.start()

    barrier = pltpu.get_barrier_semaphore()

    def greet(step, carry):
        pl.semaphore_signal(
            barrier, inc=1, device_id={"dp": lax.rem(me + step, peers)}, device_id_type=MESH
        )
        return carry

    lax.fori_loop(1, peers, greet, 0)
    for step in range(1, spans):
        pl.semaphore_signal(
            barrier, inc=1, device_id={"seq": lax.rem(shard + step, spans)}, device_id_type=MESH
        )

    dest_load.wait()
    dest = dests[...]
    is_dest = (lax.broadcasted_iota(jnp.int32, (peers, rows), 0) == dest).astype(F32)
    before = (
        lax.broadcasted_iota(jnp.int32, (rows, rows), 0)
        < lax.broadcasted_iota(jnp.int32, (rows, rows), 1)
    ).astype(F32)
    counts = dot(is_dest.astype(BF16), before.astype(BF16))
    rank = jnp.sum(is_dest * counts, axis=0, keepdims=True)
    place = dest.astype(F32) * PAD + rank
    hot = (
        lax.broadcasted_iota(jnp.int32, (padded, rows), 0).astype(F32) == place
    ).astype(F32)
    perm[...] = jnp.zeros((padded, padded), F32)
    perm[:, pl.ds(0, rows)] = hot
    perm_low = perm[...].astype(BF16)

    def exchange(phase, src, dst, first=0, last=peers - 1, beside=None):
        def one(step, carry):
            odd = lax.rem(step, 2)
            far = peers // 2 - (step + 1) // 2
            ahead = (1 - odd) * far + odd * (peers - far)
            peer = lax.rem(me + ahead, peers)
            pltpu.make_async_remote_copy(
                src_ref=src.at[pl.ds(pl.multiple_of(peer * PAD, PAD), PAD)],
                dst_ref=dst.at[pl.ds(pl.multiple_of(me * PAD, PAD), PAD)],
                send_sem=ssem.at[phase],
                recv_sem=rsem.at[phase],
                device_id={"dp": peer},
                device_id_type=MESH,
            ).start()
            if beside is not None:
                beside(step - first)
            return carry

        lax.fori_loop(first, last, one, 0)
        if first > 0:
            return
        own = pl.ds(pl.multiple_of(me * PAD, PAD), PAD)
        pltpu.make_async_copy(src.at[own], dst.at[own], rsem.at[phase]).start()

    def arrived(phase, dst):
        pltpu.make_async_copy(dst, dst, rsem.at[phase]).wait()

    def departed(phase, src):
        sent = src.at[pl.ds(0, padded - PAD)]
        pltpu.make_async_copy(sent, sent, ssem.at[phase]).wait()

    landing = (ctx.at[pl.ds(0, padded)], recvs.at[0], recvs.at[1])
    for phase in range(3):
        loads[2 * phase].wait()
        loads[2 * phase + 1].wait()
        sends[phase] = dot(perm_low, xin[:, pl.ds(phase * PAIR, PAIR)]).astype(BF16)
        if phase == 0:
            pl.semaphore_wait(barrier, peers - 1 + spans - 1)
        exchange(phase, sends.at[phase], landing[phase])

    unperm[...] = perm[...].T.astype(BF16)
    lens_load.wait()
    bounds = [lens[0, 0]]
    for entry in range(1, DOCS):
        bounds.append(bounds[-1] + lens[0, entry])

    slot_row = lax.broadcasted_iota(jnp.int32, (padded, HEAD), 0)
    column = lax.broadcasted_iota(jnp.int32, (padded, HEAD), 1)
    local = (slot_row // PAD) * group + lax.rem(slot_row, PAD)
    blank = lax.rem(slot_row, PAD) >= group

    def documents(position):
        total = jnp.zeros_like(position)
        for bound in bounds:
            total = total + (position >= bound).astype(jnp.int32)
        return total

    def spot(axis):
        index = lax.broadcasted_iota(jnp.int32, (padded, padded), axis)
        return (index // PAD) * group + lax.rem(index, PAD)

    gaps[...] = (spot(1) - spot(0)).astype(F32)

    queryf[...] = (documents(local + shard * rows) == column).astype(F32).astype(BF16)
    for back in range(spans):
        position = local + (shard - back) * rows
        shut = (documents(position) != column) | blank | (position < 0)
        keyf[pl.ds(back * padded, padded)] = jnp.where(
            shut & (column <= DOCS), NEG, 0.0
        ).astype(BF16)
    for back in range(1, spans):
        @pl.when(shard < back)
        def _():
            ctx[pl.ds(back * padded, padded)] = jnp.zeros((padded, PAIR), BF16)

    arrived(0, landing[0])

    def forward(back):
        return pltpu.make_async_remote_copy(
            src_ref=ctx.at[pl.ds(0, padded)],
            dst_ref=ctx.at[pl.ds(back * padded, padded)],
            send_sem=xssem.at[back],
            recv_sem=xrsem.at[back],
            device_id={"seq": lax.rem(shard + back, spans)},
            device_id_type=MESH,
        )

    def forwards(back):
        return shard + back < spans

    for back in range(1, spans):
        @pl.when(forwards(back))
        def _():
            forward(back).start()
    for back in range(1, spans):
        @pl.when(shard >= back)
        def _():
            forward(back).wait_recv()
    for back in range(spans):
        block = pl.ds(back * padded, padded)
        ctxt[:, block] = ctx[block, :].astype(F32).T.astype(BF16)

    def attend(member):
        arrived(1 + member, landing[1 + member])
        query = recvs[member, :, pl.ds(0, HEAD)]
        grad = recvs[member, :, pl.ds(HEAD, HEAD)]
        query_wide = jnp.concatenate([query, queryf[...]], axis=1)
        peak = None
        for back in range(spans):
            block = pl.ds(back * padded, padded)
            key_wide = jnp.concatenate([ctx[block, pl.ds(0, HEAD)], keyf[block, :]], axis=1)
            scores = dot_nt(key_wide, query_wide)
            if back == 0:
                scores = jnp.where(gaps[...] >= 0, scores, NEG)
            if back * rows + rows - 1 >= window:
                scores = jnp.where(gaps[...] < window - back * rows, scores, NEG)
            sbuf[block, :] = scores
            top = jnp.max(scores, axis=0, keepdims=True)
            peak = top if peak is None else jnp.maximum(peak, top)
        total = jnp.zeros((1, padded), F32)
        mixed = jnp.zeros((HEAD, padded), F32)
        center = jnp.zeros((1, padded), F32)
        for back in range(spans):
            block = pl.ds(back * padded, padded)
            weight = jnp.exp2((sbuf[block, :] - peak) * (SCALE * LOG2E))
            sbuf[block, :] = weight
            total = total + jnp.sum(weight, axis=0, keepdims=True)
            dprob = dot_nt(ctx[block, pl.ds(HEAD, HEAD)], grad)
            dbuf[block, :] = dprob
            center = center + jnp.sum(weight * dprob, axis=0, keepdims=True)
            mixed = mixed + dot(ctxt[pl.ds(HEAD, HEAD), block], weight.astype(BF16))
        share = 1.0 / total
        mixed = mixed * share
        center = center * share
        dquery = jnp.zeros((HEAD, padded), F32)
        for back in range(spans):
            block = pl.ds(back * padded, padded)
            prob = sbuf[block, :] * share
            dscore = (prob * (dbuf[block, :] - center)).astype(BF16)
            dquery = dquery + dot(ctxt[pl.ds(0, HEAD), block], dscore)
            for at, part in (
                (0, dot(dscore, query) * SCALE),
                (HEAD, dot(prob.astype(BF16), grad)),
            ):
                if member == 0:
                    acc[block, pl.ds(at, HEAD)] = part
                else:
                    part = acc[block, pl.ds(at, HEAD)] + part
                    gsend[back, :, pl.ds(at, HEAD)] = part.astype(BF16)
        homes[member, :, pl.ds(0, HEAD)] = mixed.T.astype(BF16)
        homes[member, :, pl.ds(HEAD, HEAD)] = (dquery * SCALE).T.astype(BF16)

    attend(0)
    exchange(3, homes.at[0], backs.at[0])
    attend(1)

    def give(back, start=0, size=padded):
        near = back < spans - 1
        start = pl.multiple_of(start, PAD)
        return pltpu.make_async_remote_copy(
            src_ref=gsend.at[back, pl.ds(start, size)],
            dst_ref=grecv.at[back, pl.ds(start, size)],
            send_sem=xssem.at[spans + back],
            recv_sem=xrsem.at[spans + back],
            device_id={"seq": lax.rem(shard + spans - (1 if near else back), spans)},
            device_id_type=MESH,
        )

    def give_on(*backs):
        def piece(index):
            for back in backs:
                @pl.when(shard >= back)
                def _():
                    give(back, index * (padded // pieces), padded // pieces).start()

        return piece

    def gets(back):
        if back < spans - 1:
            return (shard + 1 < spans) & (shard + 1 >= back)
        return shard + back < spans

    exchange(4, homes.at[1], backs.at[1], 0, pieces, give_on(spans - 1, 2))

    @pl.when(gets(2))
    def _():
        give(2).wait_recv()
        gsend[1] = (gsend[1].astype(F32) + grecv[2].astype(F32)).astype(BF16)

    rest = peers - 1 - pieces
    exchange(4, homes.at[1], backs.at[1], pieces, peers - 1, give_on(1))
    for index in range(rest, pieces):
        give_on(1)(index)
    acc[pl.ds(0, padded), :] = gsend[0].astype(F32)
    for back in (spans - 1, 1):
        @pl.when(gets(back))
        def _():
            give(back).wait_recv()
            acc[pl.ds(0, padded), :] += grecv[back].astype(F32)
    homes[2] = acc[pl.ds(0, padded), :].astype(BF16)
    exchange(5, homes.at[2], backs.at[2])

    homeward = []

    def settle(member, first, second, at):
        arrived(3 + member, backs.at[member])
        outs[member] = dot(unperm[...], backs[member]).astype(BF16)
        for half, out in enumerate((first, second)):
            store = pltpu.make_async_copy(
                outs.at[member, pl.ds(0, rows), pl.ds(half * HEAD, HEAD)],
                out.at[0, :, pl.ds(at, HEAD)],
                outsem.at[2 * member + half],
            )
            store.start()
            homeward.append(store)

    settle(0, o_ref, dq_ref, 0)
    settle(1, o_ref, dq_ref, HEAD)
    settle(2, dk_ref, dv_ref, 0)

    for phase in range(3):
        departed(phase, sends.at[phase])
        departed(3 + phase, homes.at[phase])
    for back in range(1, spans):
        @pl.when(forwards(back))
        def _():
            forward(back).wait_send()
        @pl.when(shard >= back)
        def _():
            give(back).wait_send()
    for store in homeward:
        store.wait()


def deliver(*refs):
    sources, targets, holds = refs[:4], refs[4:8], refs[8:12]
    insem, outsem = refs[12:]
    loads = [
        pltpu.make_async_copy(source, hold, insem.at[at])
        for at, (source, hold) in enumerate(zip(sources, holds))
    ]
    stores = [
        pltpu.make_async_copy(hold, target, outsem.at[at])
        for at, (hold, target) in enumerate(zip(holds, targets))
    ]
    for load in loads:
        load.start()
    for load, store in zip(loads, stores):
        load.wait()
        store.start()
    for store in stores:
        store.wait()


def solution(mesh, window=WINDOW):
    peers, spans = mesh.shape["dp"], mesh.shape["seq"]

    def local(queries, key_rows, value_rows, grad_out, doc_lengths, dest_index):
        rows = queries.shape[1]
        padded = peers * PAD
        blocks = spans * padded
        loose = pl.BlockSpec(memory_space=pl.ANY)
        shapes = tuple(
            jax.ShapeDtypeStruct((1, rows, columns), BF16) for columns in (PAIR, PAIR, HEAD, HEAD)
        )
        landed = pl.pallas_call(
            functools.partial(kernel, peers, spans, rows, window),
            out_shape=shapes,
            in_specs=[loose] * 6,
            out_specs=(loose,) * 4,
            scratch_shapes=[
                pltpu.SMEM((1, DOCS), jnp.int32),
                pltpu.VMEM((1, rows), jnp.int32),
                pltpu.VMEM((padded, 6 * HEAD), BF16),
                pltpu.VMEM((padded, padded), F32),
                pltpu.VMEM((padded, padded), BF16),
                pltpu.VMEM((3, padded, PAIR), BF16),
                pltpu.VMEM((blocks, PAIR), BF16),
                pltpu.VMEM((PAIR, blocks), BF16),
                pltpu.VMEM((2, padded, PAIR), BF16),
                pltpu.VMEM((3, padded, PAIR), BF16),
                pltpu.VMEM((3, padded, PAIR), BF16),
                pltpu.VMEM((spans, padded, PAIR), BF16),
                pltpu.VMEM((spans, padded, PAIR), BF16),
                pltpu.VMEM((blocks, PAIR), F32),
                pltpu.VMEM((blocks, padded), F32),
                pltpu.VMEM((blocks, padded), F32),
                pltpu.VMEM((padded, padded), F32),
                pltpu.VMEM((blocks, HEAD), BF16),
                pltpu.VMEM((padded, HEAD), BF16),
                pltpu.VMEM((3, padded, PAIR), BF16),
                pltpu.SemaphoreType.DMA((8,)),
                pltpu.SemaphoreType.DMA((6,)),
                pltpu.SemaphoreType.DMA((6,)),
                pltpu.SemaphoreType.DMA((6,)),
                pltpu.SemaphoreType.DMA((2 * spans,)),
                pltpu.SemaphoreType.DMA((2 * spans,)),
            ],
            compiler_params=pltpu.CompilerParams(
                collective_id=0, has_side_effects=True, vmem_limit_bytes=60 << 20
            ),
        )(queries, key_rows, value_rows, grad_out, doc_lengths, dest_index)
        return pl.pallas_call(
            deliver,
            out_shape=shapes,
            in_specs=[loose] * 4,
            out_specs=(loose,) * 4,
            scratch_shapes=[
                *(pltpu.VMEM(shape.shape, BF16) for shape in shapes),
                pltpu.SemaphoreType.DMA((4,)),
                pltpu.SemaphoreType.DMA((4,)),
            ],
        )(*landed)

    wide = P("dp", "seq", "head")
    return jax.shard_map(
        local,
        mesh=mesh,
        in_specs=(wide, wide, wide, wide, P("dp", None), P("dp", "seq")),
        out_specs=(wide, wide, wide, wide),
        check_vma=False,
    )
```

```python
import functools
import math

import jax
import jax.numpy as jnp
from jax import lax
from jax.experimental import pallas as pl
from jax.experimental.pallas import tpu as pltpu
from jax.sharding import PartitionSpec as P

HEAD = 128
PAIR = 2 * HEAD
PAD = 16
WINDOW = 1024
DOCS = 4
MIDDLE = 8
SCALE = 168.0 ** (-0.5)
LOG2E = 1.0 / math.log(2.0)
NEG = -1e30
MESH = pl.DeviceIdType.MESH
BF16 = jnp.bfloat16
F32 = jnp.float32


def dot(a, b):
    return jnp.dot(a, b, preferred_element_type=F32)


def dot_nt(a, b):
    return lax.dot_general(a, b, (((1,), (1,)), ((), ())), preferred_element_type=F32)


def kernel(peers, spans, rows, window, *refs):
    (q_ref, k_ref, v_ref, dy_ref, len_ref, dest_ref, o_ref, dq_ref, dk_ref, dv_ref,
     lens, dests, xin, perm, unperm, sends, ctx, ctxt, recvs, homes, backs, gsend, grecv, acc,
     sbuf, dbuf, gaps, keyf, queryf, outs, insem, outsem, ssem, rsem, xssem, xrsem) = refs
    me = lax.axis_index("dp")
    shard = lax.axis_index("seq")
    group = rows // peers
    padded = peers * PAD

    dest_load = pltpu.make_async_copy(dest_ref, dests, insem.at[6])
    dest_load.start()

    tail = padded - PAD * ((padded - rows + PAD - 1) // PAD)
    xin[pl.ds(tail, padded - tail), :] = jnp.zeros((padded - tail, 6 * HEAD), BF16)
    def fetch(ref, first, count, at, slot):
        return pltpu.make_async_copy(
            ref.at[0, :, pl.ds(first, count)],
            xin.at[pl.ds(0, rows), pl.ds(at, count)],
            insem.at[slot],
        )
    loads = [
        fetch(k_ref, 0, HEAD, 0, 0),
        fetch(v_ref, 0, HEAD, HEAD, 1),
        fetch(q_ref, 0, HEAD, 2 * HEAD, 2),
        fetch(dy_ref, 0, HEAD, 3 * HEAD, 3),
        fetch(q_ref, HEAD, HEAD, 4 * HEAD, 4),
        fetch(dy_ref, HEAD, HEAD, 5 * HEAD, 5),
    ]
    for load in loads:
        load.start()
    lens_load = pltpu.make_async_copy(len_ref, lens, insem.at[7])
    lens_load.start()

    barrier = pltpu.get_barrier_semaphore()

    def greet(step, carry):
        pl.semaphore_signal(
            barrier, inc=1, device_id={"dp": lax.rem(me + step, peers)}, device_id_type=MESH
        )
        return carry

    lax.fori_loop(1, peers, greet, 0)
    for step in range(1, spans):
        pl.semaphore_signal(
            barrier, inc=1, device_id={"seq": lax.rem(shard + step, spans)}, device_id_type=MESH
        )

    dest_load.wait()
    dest = dests[...]
    is_dest = (lax.broadcasted_iota(jnp.int32, (peers, rows), 0) == dest).astype(F32)
    before = (
        lax.broadcasted_iota(jnp.int32, (rows, rows), 0)
        < lax.broadcasted_iota(jnp.int32, (rows, rows), 1)
    ).astype(F32)
    counts = dot(is_dest.astype(BF16), before.astype(BF16))
    rank = jnp.sum(is_dest * counts, axis=0, keepdims=True)
    place = dest.astype(F32) * PAD + rank
    hot = (
        lax.broadcasted_iota(jnp.int32, (padded, rows), 0).astype(F32) == place
    ).astype(F32)
    perm[...] = jnp.zeros((padded, padded), F32)
    perm[:, pl.ds(0, rows)] = hot
    perm_low = perm[...].astype(BF16)

    def exchange(phase, src, dst, first=0, last=peers - 1):
        def one(step, carry):
            odd = lax.rem(step, 2)
            far = peers // 2 - (step + 1) // 2
            ahead = (1 - odd) * far + odd * (peers - far)
            peer = lax.rem(me + ahead, peers)
            pltpu.make_async_remote_copy(
                src_ref=src.at[pl.ds(pl.multiple_of(peer * PAD, PAD), PAD)],
                dst_ref=dst.at[pl.ds(pl.multiple_of(me * PAD, PAD), PAD)],
                send_sem=ssem.at[phase],
                recv_sem=rsem.at[phase],
                device_id={"dp": peer},
                device_id_type=MESH,
            ).start()
            return carry

        lax.fori_loop(first, last, one, 0)
        if first > 0:
            return
        own = pl.ds(pl.multiple_of(me * PAD, PAD), PAD)
        pltpu.make_async_copy(src.at[own], dst.at[own], rsem.at[phase]).start()

    def arrived(phase, dst):
        pltpu.make_async_copy(dst, dst, rsem.at[phase]).wait()

    def departed(phase, src):
        sent = src.at[pl.ds(0, padded - PAD)]
        pltpu.make_async_copy(sent, sent, ssem.at[phase]).wait()

    half = (pl.ds(0, HEAD), pl.ds(HEAD, HEAD))
    landing = {
        0: ctx.at[pl.ds(0, padded), half[0]],
        6: ctx.at[pl.ds(0, padded), half[1]],
        1: recvs.at[0],
        2: recvs.at[1],
    }
    leaving = {0: sends.at[0, :, half[0]], 6: sends.at[0, :, half[1]], 1: sends.at[1], 2: sends.at[2]}
    returning = {
        3: (homes.at[0, :, half[0]], backs.at[0, :, half[0]]),
        7: (homes.at[0, :, half[1]], backs.at[0, :, half[1]]),
        4: (homes.at[1], backs.at[1]),
        5: (homes.at[2, :, half[0]], backs.at[2, :, half[0]]),
        8: (homes.at[2, :, half[1]], backs.at[2, :, half[1]]),
    }
    for phase, first, count in ((0, 0, 1), (6, 1, 1), (1, 2, 2), (2, 4, 2)):
        for entry in range(first, first + count):
            loads[entry].wait()
        columns = pl.ds(first * HEAD, count * HEAD)
        leaving[phase][...] = dot(perm_low, xin[:, columns]).astype(BF16)
        if phase == 0:
            pl.semaphore_wait(barrier, peers - 1 + spans - 1)
        exchange(phase, leaving[phase], landing[phase])

    unperm[...] = perm[...].T.astype(BF16)
    lens_load.wait()
    bounds = [lens[0, 0]]
    for entry in range(1, DOCS):
        bounds.append(bounds[-1] + lens[0, entry])

    slot_row = lax.broadcasted_iota(jnp.int32, (padded, HEAD), 0)
    column = lax.broadcasted_iota(jnp.int32, (padded, HEAD), 1)
    local = (slot_row // PAD) * group + lax.rem(slot_row, PAD)
    blank = lax.rem(slot_row, PAD) >= group

    def documents(position):
        total = jnp.zeros_like(position)
        for bound in bounds:
            total = total + (position >= bound).astype(jnp.int32)
        return total

    def spot(axis):
        index = lax.broadcasted_iota(jnp.int32, (padded, padded), axis)
        return (index // PAD) * group + lax.rem(index, PAD)

    gaps[...] = (spot(1) - spot(0)).astype(F32)

    queryf[...] = (documents(local + shard * rows) == column).astype(F32).astype(BF16)
    for back in range(spans):
        position = local + (shard - back) * rows
        shut = (documents(position) != column) | blank | (position < 0)
        keyf[pl.ds(back * padded, padded)] = jnp.where(
            shut & (column <= DOCS), NEG, 0.0
        ).astype(BF16)
    for back in range(1, spans):
        @pl.when(shard < back)
        def _():
            ctx[pl.ds(back * padded, padded)] = jnp.zeros((padded, PAIR), BF16)

    def forward(back, side):
        return pltpu.make_async_remote_copy(
            src_ref=ctx.at[pl.ds(0, padded), half[side]],
            dst_ref=ctx.at[pl.ds(back * padded, padded), half[side]],
            send_sem=xssem.at[(2 * side) * spans + back],
            recv_sem=xrsem.at[(2 * side) * spans + back],
            device_id={"seq": lax.rem(shard + back, spans)},
            device_id_type=MESH,
        )

    def forwards(back):
        return shard + back < spans

    for side, phase in enumerate((0, 6)):
        arrived(phase, landing[phase])
        for back in range(1, spans):
            @pl.when(forwards(back))
            def _():
                forward(back, side).start()

    def gathered(side):
        for back in range(1, spans):
            @pl.when(shard >= back)
            def _():
                forward(back, side).wait_recv()
        for back in range(spans):
            block = pl.ds(back * padded, padded)
            ctxt[half[side], block] = ctx[block, half[side]].astype(F32).T.astype(BF16)

    def attend(member):
        if member == 0:
            gathered(0)
        arrived(1 + member, landing[1 + member])
        query = recvs[member, :, pl.ds(0, HEAD)]
        grad = recvs[member, :, pl.ds(HEAD, HEAD)]
        query_wide = jnp.concatenate([query, queryf[...]], axis=1)
        peak = None
        for back in range(spans):
            block = pl.ds(back * padded, padded)
            key_wide = jnp.concatenate([ctx[block, pl.ds(0, HEAD)], keyf[block, :]], axis=1)
            scores = dot_nt(key_wide, query_wide)
            if back == 0:
                scores = jnp.where(gaps[...] >= 0, scores, NEG)
            if back * rows + rows - 1 >= window:
                scores = jnp.where(gaps[...] < window - back * rows, scores, NEG)
            sbuf[block, :] = scores
            top = jnp.max(scores, axis=0, keepdims=True)
            peak = top if peak is None else jnp.maximum(peak, top)
        if member == 0:
            gathered(1)
        total = jnp.zeros((1, padded), F32)
        mixed = jnp.zeros((HEAD, padded), F32)
        center = jnp.zeros((1, padded), F32)
        for back in range(spans):
            block = pl.ds(back * padded, padded)
            weight = jnp.exp2((sbuf[block, :] - peak) * (SCALE * LOG2E))
            sbuf[block, :] = weight
            total = total + jnp.sum(weight, axis=0, keepdims=True)
            dprob = dot_nt(ctx[block, pl.ds(HEAD, HEAD)], grad)
            dbuf[block, :] = dprob
            center = center + jnp.sum(weight * dprob, axis=0, keepdims=True)
            mixed = mixed + dot(ctxt[pl.ds(HEAD, HEAD), block], weight.astype(BF16))
        share = 1.0 / total
        homes[member, :, pl.ds(0, HEAD)] = (mixed * share).T.astype(BF16)
        if member == 0:
            exchange(3, *returning[3])
        center = center * share
        dquery = jnp.zeros((HEAD, padded), F32)
        for back in range(spans):
            block = pl.ds(back * padded, padded)
            prob = sbuf[block, :] * share
            dscore = (prob * (dbuf[block, :] - center)).astype(BF16)
            dquery = dquery + dot(ctxt[pl.ds(0, HEAD), block], dscore)
            for at, part in (
                (0, dot(dscore, query) * SCALE),
                (HEAD, dot(prob.astype(BF16), grad)),
            ):
                if member == 0:
                    acc[block, pl.ds(at, HEAD)] = part
                else:
                    part = acc[block, pl.ds(at, HEAD)] + part
                    gsend[back, :, pl.ds(at, HEAD)] = part.astype(BF16)
        homes[member, :, pl.ds(HEAD, HEAD)] = (dquery * SCALE).T.astype(BF16)
        if member == 0:
            exchange(7, *returning[7])

    attend(0)
    attend(1)

    def give(back, side):
        near = back < spans - 1
        sem = (2 * side + 1) * spans + back
        return pltpu.make_async_remote_copy(
            src_ref=gsend.at[back, :, half[side]],
            dst_ref=grecv.at[back, :, half[side]],
            send_sem=xssem.at[sem],
            recv_sem=xrsem.at[sem],
            device_id={"seq": lax.rem(shard + spans - (1 if near else back), spans)},
            device_id_type=MESH,
        )

    def give_on(back, side):
        @pl.when(shard >= back)
        def _():
            give(back, side).start()

    def gets(back):
        if back < spans - 1:
            return (shard + 1 < spans) & (shard + 1 >= back)
        return shard + back < spans

    for side in (1, 0):
        give_on(2, side)
        give_on(spans - 1, side)
    marks = (0, MIDDLE, 2 * MIDDLE, peers - 1)
    exchange(4, *returning[4], marks[0], marks[1])
    for side in (1, 0):
        @pl.when(gets(2))
        def _():
            give(2, side).wait_recv()
            gsend[1, :, half[side]] = (
                gsend[1, :, half[side]].astype(F32) + grecv[2, :, half[side]].astype(F32)
            ).astype(BF16)

        give_on(1, side)
        exchange(4, *returning[4], marks[2 - side], marks[3 - side])
    for side in (1, 0):
        own = (pl.ds(0, padded), half[side])
        acc[own] = gsend[0, :, half[side]].astype(F32)
        for back in (spans - 1, 1):
            @pl.when(gets(back))
            def _():
                give(back, side).wait_recv()
                acc[own] += grecv[back, :, half[side]].astype(F32)
        homes[2, :, half[side]] = acc[own].astype(BF16)
        exchange(8 if side else 5, *returning[8 if side else 5])

    homeward = []

    def settle(member, phases, columns, stores):
        for phase in phases:
            arrived(phase, returning[phase][1])
        outs[member, :, columns] = dot(unperm[...], backs[member, :, columns]).astype(BF16)
        for side, out, at in stores:
            store = pltpu.make_async_copy(
                outs.at[member, pl.ds(0, rows), half[side]],
                out.at[0, :, pl.ds(at, HEAD)],
                outsem.at[2 * member + side],
            )
            store.start()
            homeward.append(store)

    both = pl.ds(0, PAIR)
    settle(0, (3, 7), both, ((0, o_ref, 0), (1, dq_ref, 0)))
    settle(1, (4,), both, ((0, o_ref, HEAD), (1, dq_ref, HEAD)))
    settle(2, (8,), half[1], ((1, dv_ref, 0),))
    settle(2, (5,), half[0], ((0, dk_ref, 0),))

    for phase, source in leaving.items():
        departed(phase, source)
    for phase, (source, _) in returning.items():
        departed(phase, source)
    for back in range(1, spans):
        @pl.when(forwards(back))
        def _():
            forward(back, 0).wait_send()
            forward(back, 1).wait_send()
        @pl.when(shard >= back)
        def _():
            give(back, 0).wait_send()
            give(back, 1).wait_send()
    for store in homeward:
        store.wait()


def deliver(*refs):
    sources, targets, holds = refs[:4], refs[4:8], refs[8:12]
    insem, outsem = refs[12:]
    loads = [
        pltpu.make_async_copy(source, hold, insem.at[at])
        for at, (source, hold) in enumerate(zip(sources, holds))
    ]
    stores = [
        pltpu.make_async_copy(hold, target, outsem.at[at])
        for at, (hold, target) in enumerate(zip(holds, targets))
    ]
    for load in loads:
        load.start()
    for load, store in zip(loads, stores):
        load.wait()
        store.start()
    for store in stores:
        store.wait()


def solution(mesh, window=WINDOW):
    peers, spans = mesh.shape["dp"], mesh.shape["seq"]

    def local(queries, key_rows, value_rows, grad_out, doc_lengths, dest_index):
        rows = queries.shape[1]
        padded = peers * PAD
        blocks = spans * padded
        loose = pl.BlockSpec(memory_space=pl.ANY)
        shapes = tuple(
            jax.ShapeDtypeStruct((1, rows, columns), BF16) for columns in (PAIR, PAIR, HEAD, HEAD)
        )
        landed = pl.pallas_call(
            functools.partial(kernel, peers, spans, rows, window),
            out_shape=shapes,
            in_specs=[loose] * 6,
            out_specs=(loose,) * 4,
            scratch_shapes=[
                pltpu.SMEM((1, DOCS), jnp.int32),
                pltpu.VMEM((1, rows), jnp.int32),
                pltpu.VMEM((padded, 6 * HEAD), BF16),
                pltpu.VMEM((padded, padded), F32),
                pltpu.VMEM((padded, padded), BF16),
                pltpu.VMEM((3, padded, PAIR), BF16),
                pltpu.VMEM((blocks, PAIR), BF16),
                pltpu.VMEM((PAIR, blocks), BF16),
                pltpu.VMEM((2, padded, PAIR), BF16),
                pltpu.VMEM((3, padded, PAIR), BF16),
                pltpu.VMEM((3, padded, PAIR), BF16),
                pltpu.VMEM((spans, padded, PAIR), BF16),
                pltpu.VMEM((spans, padded, PAIR), BF16),
                pltpu.VMEM((blocks, PAIR), F32),
                pltpu.VMEM((blocks, padded), F32),
                pltpu.VMEM((blocks, padded), F32),
                pltpu.VMEM((padded, padded), F32),
                pltpu.VMEM((blocks, HEAD), BF16),
                pltpu.VMEM((padded, HEAD), BF16),
                pltpu.VMEM((3, padded, PAIR), BF16),
                pltpu.SemaphoreType.DMA((8,)),
                pltpu.SemaphoreType.DMA((6,)),
                pltpu.SemaphoreType.DMA((9,)),
                pltpu.SemaphoreType.DMA((9,)),
                pltpu.SemaphoreType.DMA((4 * spans,)),
                pltpu.SemaphoreType.DMA((4 * spans,)),
            ],
            compiler_params=pltpu.CompilerParams(
                collective_id=0, has_side_effects=True, vmem_limit_bytes=60 << 20
            ),
        )(queries, key_rows, value_rows, grad_out, doc_lengths, dest_index)
        return pl.pallas_call(
            deliver,
            out_shape=shapes,
            in_specs=[loose] * 4,
            out_specs=(loose,) * 4,
            scratch_shapes=[
                *(pltpu.VMEM(shape.shape, BF16) for shape in shapes),
                pltpu.SemaphoreType.DMA((4,)),
                pltpu.SemaphoreType.DMA((4,)),
            ],
        )(*landed)

    wide = P("dp", "seq", "head")
    return jax.shard_map(
        local,
        mesh=mesh,
        in_specs=(wide, wide, wide, wide, P("dp", None), P("dp", "seq")),
        out_specs=(wide, wide, wide, wide),
        check_vma=False,
    )
```

```python
import functools
import math

import jax
import jax.numpy as jnp
from jax import lax
from jax.experimental import pallas as pl
from jax.experimental.pallas import tpu as pltpu
from jax.sharding import PartitionSpec as P

HEAD = 128
PAIR = 2 * HEAD
PAD = 16
WINDOW = 1024
DOCS = 4
MIDDLE = 8
SCALE = 168.0 ** (-0.5)
LOG2E = 1.0 / math.log(2.0)
NEG = -1e30
MESH = pl.DeviceIdType.MESH
BF16 = jnp.bfloat16
F32 = jnp.float32


def dot(a, b):
    return jnp.dot(a, b, preferred_element_type=F32)


def dot_nt(a, b):
    return lax.dot_general(a, b, (((1,), (1,)), ((), ())), preferred_element_type=F32)


def kernel(peers, spans, rows, window, *refs):
    (q_ref, k_ref, v_ref, dy_ref, len_ref, dest_ref, o_ref, dq_ref, dk_ref, dv_ref,
     lens, dests, xin, perm, unperm, sends, ctx, ctxt, recvs, homes, backs, gsend, grecv, acc,
     sbuf, dbuf, gaps, keyf, queryf, outs, insem, outsem, ssem, rsem, xssem, xrsem) = refs
    me = lax.axis_index("dp")
    shard = lax.axis_index("seq")
    group = rows // peers
    padded = peers * PAD

    dest_load = pltpu.make_async_copy(dest_ref, dests, insem.at[6])
    dest_load.start()

    tail = padded - PAD * ((padded - rows + PAD - 1) // PAD)
    xin[pl.ds(tail, padded - tail), :] = jnp.zeros((padded - tail, 6 * HEAD), BF16)
    def fetch(ref, first, count, at, slot):
        return pltpu.make_async_copy(
            ref.at[0, :, pl.ds(first, count)],
            xin.at[pl.ds(0, rows), pl.ds(at, count)],
            insem.at[slot],
        )
    loads = [
        fetch(k_ref, 0, HEAD, 0, 0),
        fetch(v_ref, 0, HEAD, HEAD, 1),
        fetch(q_ref, 0, HEAD, 2 * HEAD, 2),
        fetch(dy_ref, 0, HEAD, 3 * HEAD, 3),
        fetch(q_ref, HEAD, HEAD, 4 * HEAD, 4),
        fetch(dy_ref, HEAD, HEAD, 5 * HEAD, 5),
    ]
    for load in loads:
        load.start()
    lens_load = pltpu.make_async_copy(len_ref, lens, insem.at[7])
    lens_load.start()

    barrier = pltpu.get_barrier_semaphore()

    def greet(step, carry):
        pl.semaphore_signal(
            barrier, inc=1, device_id={"dp": lax.rem(me + step, peers)}, device_id_type=MESH
        )
        return carry

    lax.fori_loop(1, peers, greet, 0)
    for step in range(1, spans):
        pl.semaphore_signal(
            barrier, inc=1, device_id={"seq": lax.rem(shard + step, spans)}, device_id_type=MESH
        )

    dest_load.wait()
    dest = dests[...]
    is_dest = (lax.broadcasted_iota(jnp.int32, (peers, rows), 0) == dest).astype(F32)
    before = (
        lax.broadcasted_iota(jnp.int32, (rows, rows), 0)
        < lax.broadcasted_iota(jnp.int32, (rows, rows), 1)
    ).astype(F32)
    counts = dot(is_dest.astype(BF16), before.astype(BF16))
    rank = jnp.sum(is_dest * counts, axis=0, keepdims=True)
    place = dest.astype(F32) * PAD + rank
    hot = (
        lax.broadcasted_iota(jnp.int32, (padded, rows), 0).astype(F32) == place
    ).astype(F32)
    perm[...] = jnp.zeros((padded, padded), F32)
    perm[:, pl.ds(0, rows)] = hot
    perm_low = perm[...].astype(BF16)

    def exchange(phase, src, dst, first=0, last=peers - 1):
        def one(step, carry):
            odd = lax.rem(step, 2)
            far = peers // 2 - (step + 1) // 2
            ahead = (1 - odd) * far + odd * (peers - far)
            peer = lax.rem(me + ahead, peers)
            pltpu.make_async_remote_copy(
                src_ref=src.at[pl.ds(pl.multiple_of(peer * PAD, PAD), PAD)],
                dst_ref=dst.at[pl.ds(pl.multiple_of(me * PAD, PAD), PAD)],
                send_sem=ssem.at[phase],
                recv_sem=rsem.at[phase],
                device_id={"dp": peer},
                device_id_type=MESH,
            ).start()
            return carry

        lax.fori_loop(first, last, one, 0)
        if first > 0:
            return
        own = pl.ds(pl.multiple_of(me * PAD, PAD), PAD)
        pltpu.make_async_copy(src.at[own], dst.at[own], rsem.at[phase]).start()

    def arrived(phase, dst):
        pltpu.make_async_copy(dst, dst, rsem.at[phase]).wait()

    def departed(phase, src):
        sent = src.at[pl.ds(0, padded - PAD)]
        pltpu.make_async_copy(sent, sent, ssem.at[phase]).wait()

    half = (pl.ds(0, HEAD), pl.ds(HEAD, HEAD))
    landing = {
        0: ctx.at[pl.ds(0, padded), half[0]],
        6: ctx.at[pl.ds(0, padded), half[1]],
        1: recvs.at[0],
        2: recvs.at[1],
    }
    leaving = {0: sends.at[0, :, half[0]], 6: sends.at[0, :, half[1]], 1: sends.at[1], 2: sends.at[2]}
    returning = {
        3: (homes.at[0, :, half[0]], backs.at[0, :, half[0]]),
        7: (homes.at[0, :, half[1]], backs.at[0, :, half[1]]),
        4: (homes.at[1], backs.at[1]),
        5: (homes.at[2, :, half[0]], backs.at[2, :, half[0]]),
        8: (homes.at[2, :, half[1]], backs.at[2, :, half[1]]),
    }
    for phase, first, count in ((0, 0, 1), (6, 1, 1), (1, 2, 2), (2, 4, 2)):
        for entry in range(first, first + count):
            loads[entry].wait()
        columns = pl.ds(first * HEAD, count * HEAD)
        leaving[phase][...] = dot(perm_low, xin[:, columns]).astype(BF16)
        if phase == 0:
            pl.semaphore_wait(barrier, peers - 1 + spans - 1)
        exchange(phase, leaving[phase], landing[phase])

    unperm[...] = perm[...].T.astype(BF16)
    lens_load.wait()
    bounds = [lens[0, 0]]
    for entry in range(1, DOCS):
        bounds.append(bounds[-1] + lens[0, entry])

    slot_row = lax.broadcasted_iota(jnp.int32, (padded, HEAD), 0)
    column = lax.broadcasted_iota(jnp.int32, (padded, HEAD), 1)
    local = (slot_row // PAD) * group + lax.rem(slot_row, PAD)
    blank = lax.rem(slot_row, PAD) >= group

    def documents(position):
        total = jnp.zeros_like(position)
        for bound in bounds:
            total = total + (position >= bound).astype(jnp.int32)
        return total

    def spot(axis):
        index = lax.broadcasted_iota(jnp.int32, (padded, padded), axis)
        return (index // PAD) * group + lax.rem(index, PAD)

    gaps[...] = (spot(1) - spot(0)).astype(F32)

    queryf[...] = (documents(local + shard * rows) == column).astype(F32).astype(BF16)
    for back in range(spans):
        position = local + (shard - back) * rows
        shut = (documents(position) != column) | blank | (position < 0)
        keyf[pl.ds(back * padded, padded)] = jnp.where(
            shut & (column <= DOCS), NEG, 0.0
        ).astype(BF16)
    for back in range(1, spans):
        @pl.when(shard < back)
        def _():
            ctx[pl.ds(back * padded, padded)] = jnp.zeros((padded, PAIR), BF16)

    def forward(back, side):
        return pltpu.make_async_remote_copy(
            src_ref=ctx.at[pl.ds(0, padded), half[side]],
            dst_ref=ctx.at[pl.ds(back * padded, padded), half[side]],
            send_sem=xssem.at[(2 * side) * spans + back],
            recv_sem=xrsem.at[(2 * side) * spans + back],
            device_id={"seq": lax.rem(shard + back, spans)},
            device_id_type=MESH,
        )

    def forwards(back):
        return shard + back < spans

    for side, phase in enumerate((0, 6)):
        arrived(phase, landing[phase])
        for back in range(1, spans):
            @pl.when(forwards(back))
            def _():
                forward(back, side).start()

    def gathered(side):
        for back in range(1, spans):
            @pl.when(shard >= back)
            def _():
                forward(back, side).wait_recv()
        for back in range(spans):
            block = pl.ds(back * padded, padded)
            ctxt[half[side], block] = ctx[block, half[side]].astype(F32).T.astype(BF16)

    def give(back, side):
        near = back < spans - 1
        sem = (2 * side + 1) * spans + back
        return pltpu.make_async_remote_copy(
            src_ref=gsend.at[back, :, half[side]],
            dst_ref=grecv.at[back, :, half[side]],
            send_sem=xssem.at[sem],
            recv_sem=xrsem.at[sem],
            device_id={"seq": lax.rem(shard + spans - (1 if near else back), spans)},
            device_id_type=MESH,
        )

    def give_on(back, side):
        @pl.when(shard >= back)
        def _():
            give(back, side).start()

    def gets(back):
        if back < spans - 1:
            return (shard + 1 < spans) & (shard + 1 >= back)
        return shard + back < spans

    def attend(member):
        if member == 0:
            gathered(0)
        arrived(1 + member, landing[1 + member])
        query = recvs[member, :, pl.ds(0, HEAD)]
        grad = recvs[member, :, pl.ds(HEAD, HEAD)]
        query_wide = jnp.concatenate([query, queryf[...]], axis=1)
        peak = None
        for back in range(spans):
            block = pl.ds(back * padded, padded)
            key_wide = jnp.concatenate([ctx[block, pl.ds(0, HEAD)], keyf[block, :]], axis=1)
            scores = dot_nt(key_wide, query_wide)
            if back == 0:
                scores = jnp.where(gaps[...] >= 0, scores, NEG)
            if back * rows + rows - 1 >= window:
                scores = jnp.where(gaps[...] < window - back * rows, scores, NEG)
            sbuf[block, :] = scores
            top = jnp.max(scores, axis=0, keepdims=True)
            peak = top if peak is None else jnp.maximum(peak, top)
        if member == 0:
            gathered(1)
        total = jnp.zeros((1, padded), F32)
        mixed = jnp.zeros((HEAD, padded), F32)
        center = jnp.zeros((1, padded), F32)
        for back in range(spans):
            block = pl.ds(back * padded, padded)
            weight = jnp.exp2((sbuf[block, :] - peak) * (SCALE * LOG2E))
            sbuf[block, :] = weight
            total = total + jnp.sum(weight, axis=0, keepdims=True)
            dprob = dot_nt(ctx[block, pl.ds(HEAD, HEAD)], grad)
            dbuf[block, :] = dprob
            center = center + jnp.sum(weight * dprob, axis=0, keepdims=True)
            mixed = mixed + dot(ctxt[pl.ds(HEAD, HEAD), block], weight.astype(BF16))
        share = 1.0 / total
        homes[member, :, pl.ds(0, HEAD)] = (mixed * share).T.astype(BF16)
        if member == 0:
            exchange(3, *returning[3])
        center = center * share
        def keep(back, block, side, part):
            if member == 0:
                acc[block, half[side]] = part
            else:
                part = acc[block, half[side]] + part
                gsend[back, :, half[side]] = part.astype(BF16)

        def send_on(side):
            if member == 1:
                give_on(2, side)
                give_on(spans - 1, side)

        for back in range(spans - 1, -1, -1):
            block = pl.ds(back * padded, padded)
            prob = sbuf[block, :] * share
            sbuf[block, :] = prob
            keep(back, block, 1, dot(prob.astype(BF16), grad))
        send_on(1)
        dquery = jnp.zeros((HEAD, padded), F32)
        for back in range(spans - 1, -1, -1):
            block = pl.ds(back * padded, padded)
            dscore = (sbuf[block, :] * (dbuf[block, :] - center)).astype(BF16)
            dquery = dquery + dot(ctxt[pl.ds(0, HEAD), block], dscore)
            keep(back, block, 0, dot(dscore, query) * SCALE)
        send_on(0)
        homes[member, :, pl.ds(HEAD, HEAD)] = (dquery * SCALE).T.astype(BF16)
        if member == 0:
            exchange(7, *returning[7])

    attend(0)
    attend(1)

    marks = (0, MIDDLE, 2 * MIDDLE, peers - 1)
    exchange(4, *returning[4], marks[0], marks[1])
    for side in (1, 0):
        @pl.when(gets(2))
        def _():
            give(2, side).wait_recv()
            gsend[1, :, half[side]] = (
                gsend[1, :, half[side]].astype(F32) + grecv[2, :, half[side]].astype(F32)
            ).astype(BF16)

        give_on(1, side)
        exchange(4, *returning[4], marks[2 - side], marks[3 - side])
    for side in (1, 0):
        own = (pl.ds(0, padded), half[side])
        acc[own] = gsend[0, :, half[side]].astype(F32)
        for back in (spans - 1, 1):
            @pl.when(gets(back))
            def _():
                give(back, side).wait_recv()
                acc[own] += grecv[back, :, half[side]].astype(F32)
        homes[2, :, half[side]] = acc[own].astype(BF16)
        exchange(8 if side else 5, *returning[8 if side else 5])

    homeward = []

    def settle(member, phases, columns, stores):
        for phase in phases:
            arrived(phase, returning[phase][1])
        outs[member, :, columns] = dot(unperm[...], backs[member, :, columns]).astype(BF16)
        for side, out, at in stores:
            store = pltpu.make_async_copy(
                outs.at[member, pl.ds(0, rows), half[side]],
                out.at[0, :, pl.ds(at, HEAD)],
                outsem.at[2 * member + side],
            )
            store.start()
            homeward.append(store)

    both = pl.ds(0, PAIR)
    settle(0, (3, 7), both, ((0, o_ref, 0), (1, dq_ref, 0)))
    settle(1, (4,), both, ((0, o_ref, HEAD), (1, dq_ref, HEAD)))
    settle(2, (8,), half[1], ((1, dv_ref, 0),))
    settle(2, (5,), half[0], ((0, dk_ref, 0),))

    for phase, source in leaving.items():
        departed(phase, source)
    for phase, (source, _) in returning.items():
        departed(phase, source)
    for back in range(1, spans):
        @pl.when(forwards(back))
        def _():
            forward(back, 0).wait_send()
            forward(back, 1).wait_send()
        @pl.when(shard >= back)
        def _():
            give(back, 0).wait_send()
            give(back, 1).wait_send()
    for store in homeward:
        store.wait()


def deliver(*refs):
    sources, targets, holds = refs[:4], refs[4:8], refs[8:12]
    insem, outsem = refs[12:]
    loads = [
        pltpu.make_async_copy(source, hold, insem.at[at])
        for at, (source, hold) in enumerate(zip(sources, holds))
    ]
    stores = [
        pltpu.make_async_copy(hold, target, outsem.at[at])
        for at, (hold, target) in enumerate(zip(holds, targets))
    ]
    for load in loads:
        load.start()
    for load, store in zip(loads, stores):
        load.wait()
        store.start()
    for store in stores:
        store.wait()


def solution(mesh, window=WINDOW):
    peers, spans = mesh.shape["dp"], mesh.shape["seq"]

    def local(queries, key_rows, value_rows, grad_out, doc_lengths, dest_index):
        rows = queries.shape[1]
        padded = peers * PAD
        blocks = spans * padded
        loose = pl.BlockSpec(memory_space=pl.ANY)
        shapes = tuple(
            jax.ShapeDtypeStruct((1, rows, columns), BF16) for columns in (PAIR, PAIR, HEAD, HEAD)
        )
        landed = pl.pallas_call(
            functools.partial(kernel, peers, spans, rows, window),
            out_shape=shapes,
            in_specs=[loose] * 6,
            out_specs=(loose,) * 4,
            scratch_shapes=[
                pltpu.SMEM((1, DOCS), jnp.int32),
                pltpu.VMEM((1, rows), jnp.int32),
                pltpu.VMEM((padded, 6 * HEAD), BF16),
                pltpu.VMEM((padded, padded), F32),
                pltpu.VMEM((padded, padded), BF16),
                pltpu.VMEM((3, padded, PAIR), BF16),
                pltpu.VMEM((blocks, PAIR), BF16),
                pltpu.VMEM((PAIR, blocks), BF16),
                pltpu.VMEM((2, padded, PAIR), BF16),
                pltpu.VMEM((3, padded, PAIR), BF16),
                pltpu.VMEM((3, padded, PAIR), BF16),
                pltpu.VMEM((spans, padded, PAIR), BF16),
                pltpu.VMEM((spans, padded, PAIR), BF16),
                pltpu.VMEM((blocks, PAIR), F32),
                pltpu.VMEM((blocks, padded), F32),
                pltpu.VMEM((blocks, padded), F32),
                pltpu.VMEM((padded, padded), F32),
                pltpu.VMEM((blocks, HEAD), BF16),
                pltpu.VMEM((padded, HEAD), BF16),
                pltpu.VMEM((3, padded, PAIR), BF16),
                pltpu.SemaphoreType.DMA((8,)),
                pltpu.SemaphoreType.DMA((6,)),
                pltpu.SemaphoreType.DMA((9,)),
                pltpu.SemaphoreType.DMA((9,)),
                pltpu.SemaphoreType.DMA((4 * spans,)),
                pltpu.SemaphoreType.DMA((4 * spans,)),
            ],
            compiler_params=pltpu.CompilerParams(
                collective_id=0, has_side_effects=True, vmem_limit_bytes=60 << 20
            ),
        )(queries, key_rows, value_rows, grad_out, doc_lengths, dest_index)
        return pl.pallas_call(
            deliver,
            out_shape=shapes,
            in_specs=[loose] * 4,
            out_specs=(loose,) * 4,
            scratch_shapes=[
                *(pltpu.VMEM(shape.shape, BF16) for shape in shapes),
                pltpu.SemaphoreType.DMA((4,)),
                pltpu.SemaphoreType.DMA((4,)),
            ],
        )(*landed)

    wide = P("dp", "seq", "head")
    return jax.shard_map(
        local,
        mesh=mesh,
        in_specs=(wide, wide, wide, wide, P("dp", None), P("dp", "seq")),
        out_specs=(wide, wide, wide, wide),
        check_vma=False,
    )
```
